256 devices in a mesh: role: 4 (over y), dom: 64 (over x, z, core).
Axes of the slice: x: 4, y: 4, z: 8, core: 2. Of those that a mesh axis runs over, the one named last changes fastest.
Arguments:
- node_feats: bfloat16 [32768, 512], P(('role', 'dom')), may hold values from -6 to 6
- hub_feats: bfloat16 [1024, 512], P(('role', 'dom')), may hold values from -6 to 6
- weight: bfloat16 [1024, 512], replicated, may hold values from -0.1875 to 0.1875
- edge_src: int32 [256, 1024], P(('role', 'dom')), may hold values from 0 to 1183, as said below
- edge_dst: int32 [256, 1024], P(('role', 'dom')), may hold values from 0 to 127, as said below
- bound_rows: int32 [256, 16], P(('role', 'dom')), may hold values from 0 to 127
- hub_edge_src: int32 [256, 1024], P(('role', 'dom')), may hold values from 0 to 127
- hub_edge_slot: int32 [256, 1024], P(('role', 'dom')), may hold values from 0 to 511, as said below
- slot_hub: int32 [256, 512], P(('role', 'dom')), may hold values from 0 to 3, as said below
Outputs:
- node_out: bfloat16 [32768, 512], P(('role', 'dom'))
- hub_out: bfloat16 [1024, 512], P(('role', 'dom'))
The draws below stay inside these ranges and needn't reach their ends.
Inputs may be any that keep to these rules, and one draw needn't show every extreme that they name: `edge_src`: row indices into the source table of the device: its own nodes, then 16 rows of the device before it along dom, then 16 of the device after it, then the 1024 hubs. `edge_dst`: each node of a device is the destination of at least one of the device's edges. `hub_edge_slot`: every slot of a device receives at least one of its hub edges; slot s belongs to the owner numbered s // 2. `slot_hub`: every hub of every owner is fed by at least one slot of some device.
All inputs are finite; a program needn't handle non-finite values.
Results may differ from the reference program's by a relative error of at most 0.0027.
Values may be sent and summed in bfloat16 or wider, within the bound.
No kernel may reach another device: no remote copies, remote signals or barrier semaphores. Data moves between devices by JAX's collectives and lax.ppermute only.
A program may use at most 64 MiB of HBM per device.

```python
import jax
import jax.numpy as jnp
from jax import lax

D = 512
NODE_DEV = 128
HUB_DEV = 4
CAP = 2
E_DEV = 1024
BOUND = 16
NODES = 32768
HUBS = 1024
SLOTS = 512
HUB_EDGES = 1024
N_ROLE = 4
N_DOM = 64
DEVICES = 256


def covering_list(key, length, total):
    first_key, rest_key = jax.random.split(key)
    devices = N_ROLE * N_DOM
    first_pass = jax.vmap(lambda subkey: jax.random.permutation(subkey, length))(jax.random.split(first_key, devices))
    remaining = jax.random.randint(rest_key, (devices, total - length), 0, length)
    return jnp.concatenate([first_pass.astype(jnp.int32), remaining.astype(jnp.int32)], axis=1)


def draw_edge_src(key, part):
    devices = N_ROLE * N_DOM
    category_key, local_key, side_key, hub_key = jax.random.split(jax.random.fold_in(key, 11), 4)
    shape = (devices, E_DEV)
    category = jax.random.randint(category_key, shape, 0, 10)
    local_pick = jax.random.randint(local_key, shape, 0, NODE_DEV)
    side_pick = jax.random.randint(side_key, shape, 0, 2 * BOUND)
    hub_pick = jax.random.randint(hub_key, shape, 0, HUBS)
    chosen = jnp.where(category < 7, local_pick, jnp.where(category < 9, NODE_DEV + side_pick, NODE_DEV + 2 * BOUND + hub_pick))
    return chosen.astype(jnp.int32)


def draw_edge_dst(key, part):
    return covering_list(jax.random.fold_in(key, 23), NODE_DEV, E_DEV)


def draw_hub_edge_slot(key, part):
    return covering_list(jax.random.fold_in(key, 37), SLOTS, HUB_EDGES)


def draw_slot_hub(key, part):
    devices = N_ROLE * N_DOM
    random_key, order_key = jax.random.split(jax.random.fold_in(key, 41))
    random_hub = jax.random.randint(random_key, (devices, SLOTS), 0, HUB_DEV)
    orders = jax.vmap(lambda subkey: jax.random.permutation(subkey, devices))(jax.random.split(order_key, devices))
    source_rank = jnp.argsort(orders, axis=1, stable=True).astype(jnp.int32)
    covering = source_rank.T[:, :, None] * CAP + jnp.arange(CAP, dtype=jnp.int32)[None, None, :]
    covering = covering.reshape(devices, SLOTS)
    return jnp.where(covering < HUB_DEV, covering, random_hub).astype(jnp.int32)


def plant(values, rng, least, largest):
    longest = values.shape.index(max(values.shape))
    spots = []
    for shift in (0, 1):
        where = [jax.random.randint(jax.random.fold_in(rng, axis), (), 0, length) for axis, length in enumerate(values.shape)]
        where[longest] = (where[longest] + shift) % values.shape[longest]
        spots.append(tuple(where))
    return values.at[spots[0]].set(least).at[spots[1]].set(largest)


def level_of(key, extent, pieces, least, high):
    def one(position, shards_of):
        heights = jax.random.uniform(jax.random.fold_in(jax.random.fold_in(key, 6), position), (shards_of,), jnp.float32, least / len(pieces), high / len(pieces))
        return jnp.repeat(jnp.exp(heights), extent[position] // shards_of).reshape((-1,) + (1,) * (len(extent) - position - 1))

    factor_of = one(*pieces[0])
    for cut in pieces[1:]:
        factor_of = factor_of * one(*cut)
    return factor_of


def scatter_about(stream_key, extent, scale, bound, shards=(), held_as=jnp.bfloat16):
    result = jax.random.normal(stream_key, extent, jnp.float32) * scale
    if len(shards) > 0:
        result = level_of(stream_key, extent, shards, -0.22, 0.18) * result
    return jnp.clip(result, min=-bound, max=bound).astype(held_as)


def setup_inputs(seed: int = 0) -> dict:
    seeds = jax.random.split(jax.random.key(seed), 10)
    return {
        "node_feats": scatter_about(seeds[0], (NODES, D), 1.0, 6.0, ((0, 256),)),
        "hub_feats": scatter_about(seeds[1], (HUBS, D), 1.0, 6.0, ((0, 256),)),
        "weight": scatter_about(seeds[2], (2 * D, D), (2 * D) ** -0.5, 0.1875),
        "edge_src": draw_edge_src(jax.random.fold_in(seeds[9], 71), 0),
        "edge_dst": draw_edge_dst(jax.random.fold_in(seeds[9], 71), 0),
        "bound_rows": plant(jax.random.randint(seeds[5], (DEVICES, BOUND), 0, NODE_DEV), jax.random.fold_in(seeds[5], 1), 0, NODE_DEV - 1).astype(jnp.int32),
        "hub_edge_src": plant(jax.random.randint(seeds[6], (DEVICES, HUB_EDGES), 0, NODE_DEV), jax.random.fold_in(seeds[6], 1), 0, NODE_DEV - 1).astype(jnp.int32),
        "hub_edge_slot": draw_hub_edge_slot(jax.random.fold_in(seeds[9], 71), 0),
        "slot_hub": draw_slot_hub(jax.random.fold_in(seeds[9], 71), 0),
    }


epsilon = 1e-06

def sage_update(self_rows, mean_rows, weight):
    joined = jnp.concatenate([self_rows, mean_rows], axis=1)
    linear = jnp.dot(joined, weight, preferred_element_type=jnp.float32)
    rectified = jnp.maximum(linear, jnp.float32(0.0))
    inverse_norm = lax.rsqrt(lax.optimization_barrier(jnp.mean(rectified * rectified, axis=1, keepdims=True)) + epsilon)
    return (rectified * inverse_norm).astype(jnp.bfloat16)

def reference(node_feats, hub_feats, weight, edge_src, edge_dst, bound_rows, hub_edge_src, hub_edge_slot, slot_hub):
    devices = N_ROLE * N_DOM
    local_rows = node_feats.reshape(devices, NODE_DEV, D)
    exports = jax.vmap(lambda device_rows, picks: device_rows[picks])(local_rows, bound_rows)
    exports = exports.reshape(N_ROLE, N_DOM, BOUND, D)
    before_rows = jnp.roll(exports, 1, axis=1).reshape(devices, BOUND, D)
    after_rows = jnp.roll(exports, -1, axis=1).reshape(devices, BOUND, D)

    def one_device(operands):
        device_rows, before_part, after_part, sources, targets = operands
        source_table = jnp.concatenate([device_rows, before_part, after_part, hub_feats], axis=0)
        picked = source_table[sources].astype(jnp.float32)
        node_sum = jax.ops.segment_sum(picked, targets, num_segments=NODE_DEV)
        node_degree = jax.ops.segment_sum(jnp.ones(sources.shape, jnp.float32), targets, num_segments=NODE_DEV)
        node_mean = (node_sum / node_degree[:, None]).astype(jnp.bfloat16)
        return sage_update(device_rows, node_mean, weight)
    node_out = lax.map(one_device, (local_rows, before_rows, after_rows, edge_src, edge_dst))
    node_out = node_out.reshape(devices * NODE_DEV, D)

    def add_source(sums, operands):
        hub_sum, hub_degree = sums
        device_rows, sources, slot_ids, slot_table = operands
        hub_ids = slot_ids // CAP * HUB_DEV + slot_table[slot_ids]
        picked = device_rows[sources].astype(jnp.float32)
        hub_sum = hub_sum.at[hub_ids].add(picked)
        hub_degree = hub_degree.at[hub_ids].add(jnp.float32(1.0))
        return ((hub_sum, hub_degree), None)
    initial = (jnp.zeros((HUBS, D), jnp.float32), jnp.zeros((HUBS,), jnp.float32))
    (hub_sum, hub_degree), unused = lax.scan(add_source, initial, (local_rows, hub_edge_src, hub_edge_slot, slot_hub))
    hub_mean = (hub_sum / hub_degree[:, None]).astype(jnp.bfloat16)
    hub_out = sage_update(hub_feats, hub_mean, weight)
    return (node_out, hub_out)
```

```python
import functools

import jax
import jax.numpy as jnp
from jax import lax
from jax.experimental import pallas as pl
from jax.experimental.pallas import tpu as pltpu
from jax.sharding import Mesh
from jax.sharding import PartitionSpec as P

INNER = ("dom_1", "dom_2")
OUTER = ("role", "dom_0")
DOM = ("dom_0", "dom_1", "dom_2")
ROLE_DOM = ("role", "dom_0", "dom_1", "dom_2")

epsilon = 1e-06
F32 = jnp.float32
BF16 = jnp.bfloat16
I32 = jnp.int32
NT = (((1,), (1,)), ((), ()))
TN = (((0,), (0,)), ((), ()))
MIB = 1 << 20


def dot(a, b):
    return jnp.dot(a, b, preferred_element_type=F32)


def onehot(rows, index, first=0):
    shape = (rows, index.shape[1])
    return jnp.where(lax.broadcasted_iota(I32, shape, 0) + first == index, 1.0, 0.0).astype(BF16)


def split_count(count):
    high = jnp.floor(count * (1.0 / 256.0))
    return count - high * 256.0, high


def normalized(linear):
    rectified = jnp.maximum(linear, 0.0)
    mean = jnp.mean(rectified * rectified, axis=1, keepdims=True)
    return (rectified * lax.rsqrt(mean + epsilon)).astype(BF16)


def export_body(bound_ref, feats_ref, out_ref):
    picks = onehot(feats_ref.shape[0], bound_ref[...])
    out_ref[...] = lax.dot_general(picks, feats_ref[...], TN, preferred_element_type=F32).astype(BF16)


def slots_body(where_ref, src_ref, slot_ref, hub_ref, feats_ref, mid_ref):
    feats = feats_ref[...]
    outer = where_ref[0]
    slot = slot_ref[...]
    picks = onehot(128, src_ref[...])

    def chunk(i, carry):
        count = lax.dot_general(
            onehot(128, slot, i * 128), picks, NT, preferred_element_type=F32
        )
        low, high = split_count(count)
        sums = dot(low.astype(BF16), feats) + dot((high * 256.0).astype(BF16), feats)
        sums = sums.astype(BF16)
        for k in range(4):
            mid_ref[i * 4 + k, 32:64, :] = sums[k * 32 : (k + 1) * 32, :]
        return carry

    lax.fori_loop(0, 4, chunk, 0)
    count = lax.dot_general(
        onehot(16, slot >> 5), onehot(512, (slot & 31) + outer * 32), NT, preferred_element_type=F32
    )
    low, high = split_count(count)
    lane = lax.broadcasted_iota(I32, (1, 512), 1)
    hubs = hub_ref[...].astype(F32)
    which = (onehot(16, lane >> 5).astype(F32) * hubs).astype(BF16)
    hub = lax.dot_general(
        which, onehot(512, (lane & 31) + outer * 32), NT, preferred_element_type=F32
    )
    row = lax.broadcasted_iota(I32, (8, 512), 0)
    for t in range(16):
        about = jnp.where(row == 0, low[t : t + 1], 0.0)
        about = jnp.where(row == 1, high[t : t + 1], about)
        about = jnp.where(row == 2, hub[t : t + 1], about)
        mid_ref[t, 64:72, :] = about.astype(BF16)


def fill_body(where_ref, rows_ref, mid_in, mid_ref, wide, block, sems):
    del mid_in
    half = where_ref[1]
    for k in range(8):
        wide[4 * k : 4 * k + 4, :] = rows_ref[half * 8 + k].astype(F32)
    block[...] = wide[...].astype(BF16)
    copies = [
        pltpu.make_async_copy(block, mid_ref.at[t, pl.ds(0, 32)], sems.at[t]) for t in range(16)
    ]
    for copy in copies:
        copy.start()
    for copy in copies:
        copy.wait()


def reduce_body(mid_ref, out_ref, table_ref):
    about = jnp.zeros((8, 512), F32)
    for t in range(16):
        about = about + mid_ref[t, 64:72, :].astype(F32)
    count = about[0:1] + 256.0 * about[1:2]
    lane = lax.broadcasted_iota(I32, (1, 512), 1)
    target = ((lane & 31) >> 1) * 4 + about[2:3].astype(I32)
    picks = onehot(64, target)
    slots = mid_ref[:, 32:64, :].reshape(512, 512)
    sums = dot(picks, slots)
    degree = jnp.sum(picks.astype(F32) * count, axis=1, keepdims=True)
    low, high = split_count(degree)
    extra_lane = lax.broadcasted_iota(I32, (64, 128), 1)
    extra = jnp.where(extra_lane == 0, low, jnp.where(extra_lane == 1, high, 0.0))
    for g in range(16):
        out_ref[g, :, 0:512] = sums[4 * g : 4 * g + 4].astype(BF16)
        out_ref[g, :, 512:640] = extra[4 * g : 4 * g + 4].astype(BF16)
    table_ref[...] = mid_ref[:, 0:32, :].reshape(512, 512)


def counts_body(
    where_ref, src_ref, dst_ref, feats_ref, hub_ref, weight_ref,
    low_ref, high_ref, degree_ref, linear_ref, hub_linear_ref,
):
    half = where_ref[1]
    src = src_ref[...]
    targets = onehot(128, dst_ref[...])
    hub = src - 160
    column = 256 + (((hub >> 5) & 1) ^ half) * 512 + (hub >> 6) * 32 + (hub & 31)
    column = jnp.where(src < 160, src, column)
    degree_ref[...] = jnp.broadcast_to(
        jnp.sum(targets.astype(F32), axis=1, keepdims=True), degree_ref.shape
    )

    def chunk(i, carry):
        count = lax.dot_general(
            targets, onehot(256, column, i * 256), NT, preferred_element_type=F32
        )
        low, high = split_count(count)
        place = pl.ds(pl.multiple_of(i * 256, 256), 256)
        low_ref[:, place] = low.astype(BF16)
        high_ref[:, place] = (high * 256.0).astype(BF16)
        return carry

    lax.fori_loop(0, 5, chunk, 0)
    linear_ref[...] = dot(feats_ref[...], weight_ref[...])
    hub_linear_ref[...] = dot(hub_ref[...], weight_ref[...])


def nodes_body(
    low_ref, high_ref, degree_ref, linear_ref, feats_ref, before_ref, after_ref,
    mine_ref, other_ref, weight_ref, out_ref,
):
    def rows(ref):
        total = dot(ref[:, 0:128], feats_ref[...])
        total = total + dot(ref[:, 128:144], before_ref[...])
        total = total + dot(ref[:, 144:160], after_ref[...])
        total = total + dot(ref[:, 256:768], mine_ref[...])
        return total + dot(ref[:, 768:1280], other_ref[...])

    mean = ((rows(low_ref) + rows(high_ref)) / degree_ref[:, 0:1]).astype(BF16)
    out_ref[...] = normalized(linear_ref[...] + dot(mean, weight_ref[...]))


def hubs_body(parts_ref, linear_ref, weight_ref, out_ref):
    total = jnp.zeros((4, 640), F32)
    for g in range(16):
        total = total + parts_ref[g].astype(F32)
    degree = total[:, 512:513] + 256.0 * total[:, 513:514]
    mean = (total[:, 0:512] / degree).astype(BF16)
    out_ref[...] = normalized(linear_ref[...] + dot(mean, weight_ref[...]))


VMEM = pl.BlockSpec(memory_space=pltpu.VMEM)
SMEM = pl.BlockSpec(memory_space=pltpu.SMEM)
ANY = pl.BlockSpec(memory_space=pl.ANY)


def call(body, name, out, specs, flops, nbytes, limit=16, **more):
    out_specs = more.pop("out_specs", jax.tree.map(lambda _: VMEM, out))
    return pl.pallas_call(
        body,
        name=name,
        out_shape=out,
        in_specs=specs,
        out_specs=out_specs,
        compiler_params=pltpu.CompilerParams(vmem_limit_bytes=limit * MIB),
        cost_estimate=pl.CostEstimate(flops=flops, bytes_accessed=nbytes, transcendentals=0),
        **more,
    )


def shape(*dims, dtype=BF16):
    return jax.ShapeDtypeStruct(dims, dtype)


def on_device(
    node_feats, hub_feats, weight, edge_src, edge_dst, bound_rows,
    hub_edge_src, hub_edge_slot, slot_hub,
):
    outer = lax.axis_index(OUTER)
    where = jnp.stack([outer, lax.axis_index("dom_2")]).astype(I32)
    gathered = lax.all_to_all(
        jnp.broadcast_to(hub_feats[None], (16, 4, 512)), INNER, 0, 0, tiled=True
    )
    exports = call(export_body, "exports", shape(16, 512), [VMEM] * 2, 2 << 20, 150000)(
        bound_rows, node_feats
    )
    count = lax.axis_size(DOM)
    forward = [(i, (i + 1) % count) for i in range(count)]
    backward = [(target, source) for source, target in forward]
    before = lax.ppermute(exports, DOM, forward)
    after = lax.ppermute(exports, DOM, backward)
    mid = call(slots_body, "slots", shape(16, 72, 512), [SMEM] + [VMEM] * 4, 1 << 30, 2 << 20)(
        where, hub_edge_src, hub_edge_slot, slot_hub, node_feats
    )
    mid = call(
        fill_body, "fill", shape(16, 72, 512), [SMEM, VMEM, ANY], 0, 1 << 20,
        out_specs=ANY,
        input_output_aliases={2: 0},
        scratch_shapes=[
            pltpu.VMEM((32, 512), F32),
            pltpu.VMEM((32, 512), BF16),
            pltpu.SemaphoreType.DMA((16,)),
        ],
    )(where, gathered, mid)
    mid = lax.all_to_all(mid, OUTER, 0, 0, tiled=True)
    low, high, degree, linear, hub_linear = call(
        counts_body, "counts",
        (
            shape(128, 1280), shape(128, 1280), shape(128, 128, dtype=F32),
            shape(128, 512, dtype=F32), shape(4, 512, dtype=F32),
        ),
        [SMEM] + [VMEM] * 5, 1 << 30, 2 << 20,
    )(where, edge_src, edge_dst, node_feats, hub_feats, weight[:512])
    parts, mine = call(
        reduce_body, "reduce", (shape(16, 4, 640), shape(512, 512)), [VMEM], 1 << 26, 2 << 20
    )(mid)
    other = lax.ppermute(mine, "dom_2", [(0, 1), (1, 0)])
    parts = lax.all_to_all(parts, INNER, 0, 0, tiled=True)
    node_out = call(nodes_body, "nodes", shape(128, 512), [VMEM] * 10, 1 << 29, 2 << 20)(
        low, high, degree, linear, node_feats, before, after, mine, other, weight[512:]
    )
    hub_out = call(hubs_body, "hubs", shape(4, 512), [VMEM] * 3, 1 << 22, 1 << 19)(
        parts, hub_linear, weight[512:]
    )
    return (node_out, hub_out)


def solution(mesh):
    finer = Mesh(mesh.devices.reshape(4, 4, 8, 2), ROLE_DOM)
    rows = P(ROLE_DOM, None)
    in_specs = (rows, rows, P(), rows, rows, rows, rows, rows, rows)
    return jax.shard_map(
        on_device, mesh=finer, in_specs=in_specs, out_specs=(rows, rows), check_vma=False
    )
```

```python
import jax
import jax.numpy as jnp
from jax import lax
from jax.experimental import pallas as pl
from jax.experimental.pallas import tpu as pltpu
from jax.sharding import Mesh
from jax.sharding import PartitionSpec as P


INNER = ("dom_1", "dom_2")
OUTER = ("role", "dom_0")
DOM = ("dom_0", "dom_1", "dom_2")
ROLE_DOM = ("role", "dom_0", "dom_1", "dom_2")

epsilon = 1e-06
F32 = jnp.float32
BF16 = jnp.bfloat16
I32 = jnp.int32
NT = (((1,), (1,)), ((), ()))
TN = (((0,), (0,)), ((), ()))
MIB = 1 << 20


def dot(a, b):
    return jnp.dot(a, b, preferred_element_type=F32)


def onehot(rows, index, first=0):
    shape = (rows, index.shape[1])
    return jnp.where(lax.broadcasted_iota(I32, shape, 0) + first == index, 1.0, 0.0).astype(BF16)


def split_count(count):
    high = jnp.floor(count * (1.0 / 256.0))
    return count - high * 256.0, high


def normalized(linear):
    rectified = jnp.maximum(linear, 0.0)
    mean = jnp.mean(rectified * rectified, axis=1, keepdims=True)
    return (rectified * lax.rsqrt(mean + epsilon)).astype(BF16)


def spread_body(rows_ref, out_ref, sems):
    copies = [
        pltpu.make_async_copy(rows_ref, out_ref.at[k], sems.at[k]) for k in range(out_ref.shape[0])
    ]
    for copy in copies:
        copy.start()
    for copy in copies:
        copy.wait()


def export_body(bound_ref, feats_ref, out_ref):
    picks = onehot(feats_ref.shape[0], bound_ref[...])
    out_ref[...] = lax.dot_general(picks, feats_ref[...], TN, preferred_element_type=F32).astype(BF16)


def slots_body(
    where_ref, src_hbm, slot_hbm, hub_hbm, feats_hbm, mid_ref,
    src_ref, slot_ref, hub_ref, feats_ref, sems,
):
    copies = [
        pltpu.make_async_copy(source, target, sems.at[k])
        for k, (source, target) in enumerate(
            ((src_hbm, src_ref), (slot_hbm, slot_ref), (hub_hbm, hub_ref), (feats_hbm, feats_ref))
        )
    ]
    for copy in copies:
        copy.start()
    for copy in copies:
        copy.wait()
    feats = feats_ref[...]
    outer = where_ref[0]
    slot = slot_ref[...]
    picks = onehot(128, src_ref[...])

    def chunk(i, carry):
        count = lax.dot_general(
            onehot(128, slot, i * 128), picks, NT, preferred_element_type=F32
        )
        low, high = split_count(count)
        sums = dot(low.astype(BF16), feats) + dot((high * 256.0).astype(BF16), feats)
        sums = sums.astype(BF16)
        for k in range(4):
            mid_ref[i * 4 + k, 32:64, :] = sums[k * 32 : (k + 1) * 32, :]
        return carry

    lax.fori_loop(0, 4, chunk, 0)
    count = lax.dot_general(
        onehot(16, slot >> 5), onehot(512, (slot & 31) + outer * 32), NT, preferred_element_type=F32
    )
    low, high = split_count(count)
    lane = lax.broadcasted_iota(I32, (1, 512), 1)
    hubs = hub_ref[...].astype(F32)
    which = (onehot(16, lane >> 5).astype(F32) * hubs).astype(BF16)
    hub = lax.dot_general(
        which, onehot(512, (lane & 31) + outer * 32), NT, preferred_element_type=F32
    )
    row = lax.broadcasted_iota(I32, (8, 512), 0)
    for t in range(16):
        about = jnp.where(row == 0, low[t : t + 1], 0.0)
        about = jnp.where(row == 1, high[t : t + 1], about)
        about = jnp.where(row == 2, hub[t : t + 1], about)
        mid_ref[t, 64:72, :] = about.astype(BF16)


def fill_body(where_ref, rows_ref, mid_in, mid_ref, wide, block, sems):
    del mid_in
    half = where_ref[1]
    for k in range(8):
        wide[4 * k : 4 * k + 4, :] = rows_ref[half * 8 + k].astype(F32)
    block[...] = wide[...].astype(BF16)
    copies = [
        pltpu.make_async_copy(block, mid_ref.at[t, pl.ds(0, 32)], sems.at[t]) for t in range(16)
    ]
    for copy in copies:
        copy.start()
    for copy in copies:
        copy.wait()


def reduce_body(mid_ref, out_hbm, table_ref, out_ref, sem):
    about = jnp.zeros((8, 512), F32)
    for t in range(16):
        about = about + mid_ref[t, 64:72, :].astype(F32)
    count = about[0:1] + 256.0 * about[1:2]
    lane = lax.broadcasted_iota(I32, (1, 512), 1)
    target = ((lane & 31) >> 1) * 4 + about[2:3].astype(I32)
    picks = onehot(64, target)
    slots = mid_ref[:, 32:64, :].reshape(512, 512)
    sums = dot(picks, slots)
    degree = jnp.sum(picks.astype(F32) * count, axis=1, keepdims=True)
    low, high = split_count(degree)
    extra_lane = lax.broadcasted_iota(I32, (64, 128), 1)
    extra = jnp.where(extra_lane == 0, low, jnp.where(extra_lane == 1, high, 0.0))
    for g in range(16):
        out_ref[g, :, 0:512] = sums[4 * g : 4 * g + 4].astype(BF16)
        out_ref[g, :, 512:640] = extra[4 * g : 4 * g + 4].astype(BF16)
    copy = pltpu.make_async_copy(out_ref, out_hbm, sem)
    copy.start()
    table_ref[...] = mid_ref[:, 0:32, :].reshape(512, 512)
    copy.wait()


def counts_body(
    where_ref, src_ref, dst_ref, feats_ref, before_ref, after_ref, hub_ref, weight_ref,
    low_ref, high_ref, degree_ref, partial_ref, hub_linear_ref,
):
    half = where_ref[1]
    src = src_ref[...]
    targets = onehot(128, dst_ref[...])
    hub = src - 160
    column = (((hub >> 5) & 1) ^ half) * 512 + (hub >> 6) * 32 + (hub & 31)
    column = jnp.where(hub < 0, -1, column)
    degree_ref[...] = jnp.broadcast_to(
        jnp.sum(targets.astype(F32), axis=1, keepdims=True), degree_ref.shape
    )

    def counted(index, first):
        count = lax.dot_general(
            targets, onehot(256, index, first), NT, preferred_element_type=F32
        )
        low, high = split_count(count)
        return low.astype(BF16), (high * 256.0).astype(BF16)

    def chunk(i, carry):
        low, high = counted(column, i * 256)
        place = pl.ds(pl.multiple_of(i * 256, 256), 256)
        low_ref[:, place] = low
        high_ref[:, place] = high
        return carry

    lax.fori_loop(0, 4, chunk, 0)
    total = jnp.zeros((128, 512), F32)
    for part in counted(src, 0):
        total = total + dot(part[:, 0:128], feats_ref[...])
        total = total + dot(part[:, 128:144], before_ref[...])
        total = total + dot(part[:, 144:160], after_ref[...])
    partial_ref[...] = total
    hub_linear_ref[...] = dot(hub_ref[...], weight_ref[0:512])


def nodes_body(
    low_ref, high_ref, degree_ref, partial_ref, feats_ref, mine_ref, other_ref, weight_ref, out_ref
):
    linear = dot(feats_ref[...], weight_ref[0:512])
    total = partial_ref[...]
    for ref in (low_ref, high_ref):
        total = total + dot(ref[:, 0:512], mine_ref[...])
        total = total + dot(ref[:, 512:1024], other_ref[...])
    mean = (total / degree_ref[:, 0:1]).astype(BF16)
    out_ref[...] = normalized(linear + dot(mean, weight_ref[512:1024]))


def hubs_body(parts_ref, linear_ref, weight_ref, out_ref):
    total = jnp.zeros((4, 640), F32)
    for g in range(16):
        total = total + parts_ref[g].astype(F32)
    degree = total[:, 512:513] + 256.0 * total[:, 513:514]
    mean = (total[:, 0:512] / degree).astype(BF16)
    out_ref[...] = normalized(linear_ref[...] + dot(mean, weight_ref[512:1024]))


VMEM = pl.BlockSpec(memory_space=pltpu.VMEM)
SMEM = pl.BlockSpec(memory_space=pltpu.SMEM)
ANY = pl.BlockSpec(memory_space=pl.ANY)
HBM = pl.BlockSpec(memory_space=pltpu.HBM)


def call(body, out, specs, flops, nbytes, limit=16, **more):
    out_specs = more.pop("out_specs", jax.tree.map(lambda _: VMEM, out))
    return pl.pallas_call(
        body,
        out_shape=out,
        in_specs=specs,
        out_specs=out_specs,
        compiler_params=pltpu.CompilerParams(vmem_limit_bytes=limit * MIB),
        cost_estimate=pl.CostEstimate(flops=flops, bytes_accessed=nbytes, transcendentals=0),
        **more,
    )


def shape(*dims, dtype=BF16):
    return jax.ShapeDtypeStruct(dims, dtype)


def in_hbm(*arrays):
    return [pltpu.with_memory_space_constraint(a, pltpu.HBM) for a in arrays]


def on_device(
    node_feats, hub_feats, weight, edge_src, edge_dst, bound_rows,
    hub_edge_src, hub_edge_slot, slot_hub,
):
    outer = lax.axis_index(OUTER)
    where = jnp.stack([outer, lax.axis_index("dom_2")]).astype(I32)
    spread = call(
        spread_body, pltpu.HBM((16, 4, 512), BF16), [HBM], 0, 70000,
        out_specs=HBM,
        scratch_shapes=[pltpu.SemaphoreType.DMA((16,))],
    )(*in_hbm(hub_feats))
    gathered = lax.all_to_all(spread, INNER, 0, 0, tiled=True)
    mid = call(
        slots_body, shape(16, 72, 512), [SMEM] + [HBM] * 4, 1 << 30, 2 << 20,
        scratch_shapes=[
            pltpu.VMEM((1, 1024), I32),
            pltpu.VMEM((1, 1024), I32),
            pltpu.VMEM((1, 512), I32),
            pltpu.VMEM((128, 512), BF16),
            pltpu.SemaphoreType.DMA((4,)),
        ],
    )(where, *in_hbm(hub_edge_src, hub_edge_slot, slot_hub, node_feats))
    mid = call(
        fill_body, shape(16, 72, 512), [SMEM, VMEM, ANY], 0, 1 << 20,
        out_specs=ANY,
        input_output_aliases={2: 0},
        scratch_shapes=[
            pltpu.VMEM((32, 512), F32),
            pltpu.VMEM((32, 512), BF16),
            pltpu.SemaphoreType.DMA((16,)),
        ],
    )(where, gathered, mid)
    mid = lax.all_to_all(mid, OUTER, 0, 0, tiled=True)
    exports = call(export_body, shape(16, 512), [VMEM] * 2, 2 << 20, 150000)(bound_rows, node_feats)
    count = lax.axis_size(DOM)
    forward = [(i, (i + 1) % count) for i in range(count)]
    backward = [(target, source) for source, target in forward]
    before = lax.ppermute(exports, DOM, forward)
    after = lax.ppermute(exports, DOM, backward)
    low, high, degree, partial, hub_linear = call(
        counts_body,
        (
            shape(128, 1024), shape(128, 1024), shape(128, 128, dtype=F32),
            shape(128, 512, dtype=F32), shape(4, 512, dtype=F32),
        ),
        [SMEM] + [VMEM] * 7, 1 << 30, 2 << 20,
    )(where, edge_src, edge_dst, node_feats, before, after, hub_feats, weight)
    parts, mine = call(
        reduce_body, (pltpu.HBM((16, 4, 640), BF16), shape(512, 512)), [VMEM],
        1 << 26, 2 << 20,
        out_specs=(HBM, VMEM),
        scratch_shapes=[pltpu.VMEM((16, 4, 640), BF16), pltpu.SemaphoreType.DMA],
    )(mid)
    parts = lax.all_to_all(parts, INNER, 0, 0, tiled=True)
    other = lax.ppermute(mine, "dom_2", [(0, 1), (1, 0)])
    node_out = call(nodes_body, shape(128, 512), [VMEM] * 8, 1 << 29, 2 << 20)(
        low, high, degree, partial, node_feats, mine, other, weight
    )
    hub_out = call(hubs_body, shape(4, 512), [VMEM] * 3, 1 << 22, 1 << 19)(
        parts, hub_linear, weight
    )
    return (node_out, hub_out)


def solution(mesh):
    finer = Mesh(mesh.devices.reshape(4, 4, 8, 2), ROLE_DOM)
    rows = P(ROLE_DOM, None)
    in_specs = (rows, rows, P(), rows, rows, rows, rows, rows, rows)
    return jax.shard_map(
        on_device, mesh=finer, in_specs=in_specs, out_specs=(rows, rows), check_vma=False
    )
```

```python
import jax
import jax.numpy as jnp
from jax import lax
from jax.experimental import pallas as pl
from jax.experimental.pallas import tpu as pltpu
from jax.sharding import Mesh
from jax.sharding import PartitionSpec as P


INNER = ("dom_1", "dom_2")
OUTER = ("role", "dom_0")
DOM = ("dom_0", "dom_1", "dom_2")
ROLE_DOM = ("role", "dom_0", "dom_1", "dom_2")

epsilon = 1e-06
F32 = jnp.float32
BF16 = jnp.bfloat16
I32 = jnp.int32
NT = (((1,), (1,)), ((), ()))
TN = (((0,), (0,)), ((), ()))
MIB = 1 << 20


def dot(a, b):
    return jnp.dot(a, b, preferred_element_type=F32)


def onehot(rows, index, first=0):
    shape = (rows, index.shape[1])
    return jnp.where(lax.broadcasted_iota(I32, shape, 0) + first == index, 1.0, 0.0).astype(BF16)


def split_count(count):
    high = jnp.floor(count * (1.0 / 256.0))
    return count - high * 256.0, high


def normalized(linear):
    rectified = jnp.maximum(linear, 0.0)
    mean = jnp.mean(rectified * rectified, axis=1, keepdims=True)
    return (rectified * lax.rsqrt(mean + epsilon)).astype(BF16)


def export_body(bound_ref, feats_ref, out_ref):
    picks = onehot(feats_ref.shape[0], bound_ref[...])
    out_ref[...] = lax.dot_general(picks, feats_ref[...], TN, preferred_element_type=F32).astype(BF16)


def repeated(index):
    shape = (128, index.shape[1])
    row = lax.broadcasted_iota(I32, shape, 0) & 31
    return jnp.where(row == index, 1.0, 0.0).astype(BF16)


GATHERED, SLOTS, ABOUT, ROWS = 0, 128, 256, 264


def block_of(first, k):
    return pl.ds(first + 32 * k, 32)


def slots_body(
    src_hbm, slot_hbm, hub_hbm, feats_hbm, mid_ref,
    src_ref, slot_ref, hub_ref, feats_ref, sems,
):
    copies = [
        pltpu.make_async_copy(source, target, sems.at[k])
        for k, (source, target) in enumerate(
            ((src_hbm, src_ref), (slot_hbm, slot_ref), (hub_hbm, hub_ref), (feats_hbm, feats_ref))
        )
    ]
    for copy in copies:
        copy.start()
    for copy in copies:
        copy.wait()
    feats = feats_ref[...]
    slot = slot_ref[...]
    picks = onehot(128, src_ref[...])

    def chunk(i, carry):
        count = lax.dot_general(
            onehot(128, slot, i * 128), picks, NT, preferred_element_type=F32
        )
        low, high = split_count(count)
        sums = dot(low.astype(BF16), feats) + dot((high * 256.0).astype(BF16), feats)
        sums = sums.astype(BF16)
        for t in range(4):
            for k in range(4):
                mid_ref[i * 4 + t, block_of(SLOTS, k), :] = sums[
                    t * 32 : (t + 1) * 32, k * 128 : (k + 1) * 128
                ]
        return carry

    lax.fori_loop(0, 4, chunk, 0)
    count = lax.dot_general(
        onehot(16, slot >> 5), repeated(slot & 31), NT, preferred_element_type=F32
    )
    low, high = split_count(count)
    lane = lax.broadcasted_iota(I32, (1, 512), 1)
    hubs = hub_ref[...].astype(F32)
    which = (onehot(16, lane >> 5).astype(F32) * hubs).astype(BF16)
    hub = lax.dot_general(which, repeated(lane & 31), NT, preferred_element_type=F32)
    row = lax.broadcasted_iota(I32, (8, 128), 0)
    for t in range(16):
        about = jnp.where(row == 0, low[t : t + 1], 0.0)
        about = jnp.where(row == 1, high[t : t + 1], about)
        about = jnp.where(row == 2, hub[t : t + 1], about)
        mid_ref[t, ABOUT:ROWS, :] = about.astype(BF16)


def fill_body(rows_ref, mid_in, mid_ref, wide, block, sems):
    del mid_in
    for z in range(8):
        wide[4 * z : 4 * z + 4, :] = rows_ref[z].astype(F32)
    for k in range(4):
        block[32 * k : 32 * k + 32, :] = wide[:, 128 * k : 128 * k + 128].astype(BF16)
    copies = [
        pltpu.make_async_copy(block, mid_ref.at[t, pl.ds(GATHERED, 128)], sems.at[t])
        for t in range(16)
    ]
    for copy in copies:
        copy.start()
    for copy in copies:
        copy.wait()


def reduce_body(mid_ref, out_hbm, table_ref, out_ref, sem):
    lane = lax.broadcasted_iota(I32, (8, 128), 1)
    blocks = []
    for k in range(4):
        block = jnp.zeros((8, 128), F32)
        for i in range(4):
            block = jnp.where(lane >> 5 == i, mid_ref[4 * k + i, ABOUT:ROWS, :].astype(F32), block)
        blocks.append(block)
    about = jnp.concatenate(blocks, axis=1)
    count = about[0:1] + 256.0 * about[1:2]
    lane = lax.broadcasted_iota(I32, (1, 512), 1)
    target = ((lane & 31) >> 1) * 4 + about[2:3].astype(I32)
    picks = onehot(64, target)
    slots = [mid_ref[:, block_of(SLOTS, k), :].reshape(512, 128) for k in range(4)]
    sums = dot(picks, jnp.concatenate(slots, axis=1))
    degree = jnp.sum(picks.astype(F32) * count, axis=1, keepdims=True)
    low, high = split_count(degree)
    extra_lane = lax.broadcasted_iota(I32, (64, 128), 1)
    extra = jnp.where(extra_lane == 0, low, jnp.where(extra_lane == 1, high, 0.0))
    for g in range(16):
        out_ref[g, :, 0:512] = sums[4 * g : 4 * g + 4].astype(BF16)
        out_ref[g, :, 512:640] = extra[4 * g : 4 * g + 4].astype(BF16)
    copy = pltpu.make_async_copy(out_ref, out_hbm, sem)
    copy.start()
    for k in range(4):
        table_ref[:, 128 * k : 128 * k + 128] = mid_ref[:, block_of(GATHERED, k), :].reshape(512, 128)
    copy.wait()


def counts_body(
    where_ref, src_ref, dst_ref, feats_ref, before_ref, after_ref, hub_ref, weight_ref,
    low_ref, high_ref, degree_ref, hub_linear_ref, partial_hbm, partial_ref, sem,
):
    half = where_ref[0]
    src = src_ref[...]
    targets = onehot(128, dst_ref[...])
    hub = src - 160
    column = (((hub >> 2) & 1) ^ half) * 512 + (hub >> 6) * 32 + ((hub & 56) >> 1) + (hub & 3)
    column = jnp.where(hub < 0, -1, column)
    degree_ref[...] = jnp.broadcast_to(
        jnp.sum(targets.astype(F32), axis=1, keepdims=True), degree_ref.shape
    )

    def counted(index, first):
        count = lax.dot_general(
            targets, onehot(256, index, first), NT, preferred_element_type=F32
        )
        low, high = split_count(count)
        return low.astype(BF16), (high * 256.0).astype(BF16)

    def chunk(i, carry):
        low, high = counted(column, i * 256)
        place = pl.ds(pl.multiple_of(i * 256, 256), 256)
        low_ref[:, place] = low
        high_ref[:, place] = high
        return carry

    lax.fori_loop(0, 4, chunk, 0)
    total = jnp.zeros((128, 512), F32)
    for part in counted(src, 0):
        total = total + dot(part[:, 0:128], feats_ref[...])
        total = total + dot(part[:, 128:144], before_ref[...])
        total = total + dot(part[:, 144:160], after_ref[...])
    partial_ref[...] = total
    copy = pltpu.make_async_copy(partial_ref, partial_hbm, sem)
    copy.start()
    hub_linear_ref[...] = dot(hub_ref[...], weight_ref[0:512])
    copy.wait()


def nodes_body(
    low_ref, high_ref, degree_ref, partial_hbm, feats_ref, mine_ref, other_ref, weight_ref, out_ref,
    partial_ref, sem,
):
    copy = pltpu.make_async_copy(partial_hbm, partial_ref, sem)
    copy.start()
    linear = dot(feats_ref[...], weight_ref[0:512])
    total = jnp.zeros((128, 512), F32)
    for ref in (low_ref, high_ref):
        total = total + dot(ref[:, 0:512], mine_ref[...])
        total = total + dot(ref[:, 512:1024], other_ref[...])
    copy.wait()
    total = total + partial_ref[...]
    mean = (total / degree_ref[:, 0:1]).astype(BF16)
    out_ref[...] = normalized(linear + dot(mean, weight_ref[512:1024]))


def hubs_body(parts_ref, linear_ref, weight_ref, out_ref):
    total = jnp.zeros((4, 640), F32)
    for g in range(16):
        total = total + parts_ref[g].astype(F32)
    degree = total[:, 512:513] + 256.0 * total[:, 513:514]
    mean = (total[:, 0:512] / degree).astype(BF16)
    out_ref[...] = normalized(linear_ref[...] + dot(mean, weight_ref[512:1024]))


VMEM = pl.BlockSpec(memory_space=pltpu.VMEM)
SMEM = pl.BlockSpec(memory_space=pltpu.SMEM)
ANY = pl.BlockSpec(memory_space=pl.ANY)
HBM = pl.BlockSpec(memory_space=pltpu.HBM)


def call(body, out, specs, flops, nbytes, limit=16, **more):
    out_specs = more.pop("out_specs", jax.tree.map(lambda _: VMEM, out))
    return pl.pallas_call(
        body,
        out_shape=out,
        in_specs=specs,
        out_specs=out_specs,
        compiler_params=pltpu.CompilerParams(vmem_limit_bytes=limit * MIB),
        cost_estimate=pl.CostEstimate(flops=flops, bytes_accessed=nbytes, transcendentals=0),
        **more,
    )


def shape(*dims, dtype=BF16):
    return jax.ShapeDtypeStruct(dims, dtype)


def in_hbm(*arrays):
    return [pltpu.with_memory_space_constraint(a, pltpu.HBM) for a in arrays]


def on_device(
    node_feats, hub_feats, weight, edge_src, edge_dst, bound_rows,
    hub_edge_src, hub_edge_slot, slot_hub,
):
    where = lax.axis_index("dom_2").astype(I32).reshape(1)
    gathered = lax.all_to_all(
        jnp.broadcast_to(hub_feats[None], (8, 4, 512)), "dom_1", 0, 0, tiled=True
    )
    mid = call(
        slots_body, shape(16, ROWS, 128), [HBM] * 4, 1 << 30, 2 << 20,
        scratch_shapes=[
            pltpu.VMEM((1, 1024), I32),
            pltpu.VMEM((1, 1024), I32),
            pltpu.VMEM((1, 512), I32),
            pltpu.VMEM((128, 512), BF16),
            pltpu.SemaphoreType.DMA((4,)),
        ],
    )(*in_hbm(hub_edge_src, hub_edge_slot, slot_hub, node_feats))
    mid = call(
        fill_body, shape(16, ROWS, 128), [VMEM, ANY], 0, 1 << 20,
        out_specs=ANY,
        input_output_aliases={1: 0},
        scratch_shapes=[
            pltpu.VMEM((32, 512), F32),
            pltpu.VMEM((128, 128), BF16),
            pltpu.SemaphoreType.DMA((16,)),
        ],
    )(gathered, mid)
    mid = lax.all_to_all(mid, OUTER, 0, 0, tiled=True)
    exports = call(export_body, shape(16, 512), [VMEM] * 2, 2 << 20, 150000)(bound_rows, node_feats)
    count = lax.axis_size(DOM)
    forward = [(i, (i + 1) % count) for i in range(count)]
    backward = [(target, source) for source, target in forward]
    before = lax.ppermute(exports, DOM, forward)
    after = lax.ppermute(exports, DOM, backward)
    low, high, degree, hub_linear, partial = call(
        counts_body,
        (
            shape(128, 1024), shape(128, 1024), shape(128, 128, dtype=F32),
            shape(4, 512, dtype=F32), pltpu.HBM((128, 512), F32),
        ),
        [SMEM] + [VMEM] * 7, 1 << 30, 2 << 20,
        out_specs=(VMEM, VMEM, VMEM, VMEM, HBM),
        scratch_shapes=[pltpu.VMEM((128, 512), F32), pltpu.SemaphoreType.DMA],
    )(where, edge_src, edge_dst, node_feats, before, after, hub_feats, weight)
    parts, mine = call(
        reduce_body, (pltpu.HBM((16, 4, 640), BF16), shape(512, 512)), [VMEM],
        1 << 26, 2 << 20,
        out_specs=(HBM, VMEM),
        scratch_shapes=[pltpu.VMEM((16, 4, 640), BF16), pltpu.SemaphoreType.DMA],
    )(mid)
    parts = lax.all_to_all(parts, INNER, 0, 0, tiled=True)
    other = lax.ppermute(mine, "dom_2", [(0, 1), (1, 0)])
    node_out = call(
        nodes_body, shape(128, 512), [VMEM] * 3 + [HBM] + [VMEM] * 4, 1 << 29, 2 << 20,
        scratch_shapes=[pltpu.VMEM((128, 512), F32), pltpu.SemaphoreType.DMA],
    )(low, high, degree, *in_hbm(partial), node_feats, mine, other, weight)
    hub_out = call(hubs_body, shape(4, 512), [VMEM] * 3, 1 << 22, 1 << 19)(
        parts, hub_linear, weight
    )
    return (node_out, hub_out)


def solution(mesh):
    finer = Mesh(mesh.devices.reshape(4, 4, 8, 2), ROLE_DOM)
    rows = P(ROLE_DOM, None)
    in_specs = (rows, rows, P(), rows, rows, rows, rows, rows, rows)
    return jax.shard_map(
        on_device, mesh=finer, in_specs=in_specs, out_specs=(rows, rows), check_vma=False
    )
```

```python
import jax
import jax.numpy as jnp
from jax import lax
from jax.experimental import pallas as pl
from jax.experimental.pallas import tpu as pltpu
from jax.sharding import Mesh
from jax.sharding import PartitionSpec as P


INNER = ("pair", "side", "core")
OUTER = ("role", "x")
DOM = ("x", "pair", "side", "core")
ROLE_DOM = ("role", "x", "pair", "side", "core")

epsilon = 1e-06
F32 = jnp.float32
BF16 = jnp.bfloat16
I32 = jnp.int32
NT = (((1,), (1,)), ((), ()))
TN = (((0,), (0,)), ((), ()))
MIB = 1 << 20


def dot(a, b):
    return jnp.dot(a, b, preferred_element_type=F32)


def onehot(rows, index, first=0):
    shape = (rows, index.shape[1])
    return jnp.where(lax.broadcasted_iota(I32, shape, 0) + first == index, 1.0, 0.0).astype(BF16)


def split_count(count):
    high = jnp.floor(count * (1.0 / 256.0))
    return count - high * 256.0, high


def normalized(linear):
    rectified = jnp.maximum(linear, 0.0)
    mean = jnp.mean(rectified * rectified, axis=1, keepdims=True)
    return (rectified * lax.rsqrt(mean + epsilon)).astype(BF16)


def export_body(bound_ref, feats_ref, out_ref):
    picks = onehot(feats_ref.shape[0], bound_ref[...])
    out_ref[...] = lax.dot_general(picks, feats_ref[...], TN, preferred_element_type=F32).astype(BF16)


def repeated(index):
    shape = (128, index.shape[1])
    row = lax.broadcasted_iota(I32, shape, 0) & 31
    return jnp.where(row == index, 1.0, 0.0).astype(BF16)


GATHERED, SLOTS, ABOUT, ROWS = 0, 64, 192, 200


def block_of(first, k):
    size = (SLOTS if first == GATHERED else ABOUT - SLOTS) // 4
    return pl.ds(first + size * k, size)


def slots_body(
    src_hbm, slot_hbm, hub_hbm, feats_hbm, mid_ref,
    src_ref, slot_ref, hub_ref, feats_ref, sems,
):
    copies = [
        pltpu.make_async_copy(source, target, sems.at[k])
        for k, (source, target) in enumerate(
            ((src_hbm, src_ref), (slot_hbm, slot_ref), (hub_hbm, hub_ref), (feats_hbm, feats_ref))
        )
    ]
    for copy in copies:
        copy.start()
    for copy in copies:
        copy.wait()
    feats = feats_ref[...]
    slot = slot_ref[...]
    picks = onehot(128, src_ref[...])

    def chunk(i, carry):
        count = lax.dot_general(
            onehot(128, slot, i * 128), picks, NT, preferred_element_type=F32
        )
        low, high = split_count(count)
        sums = dot(low.astype(BF16), feats) + dot((high * 256.0).astype(BF16), feats)
        sums = sums.astype(BF16)
        for t in range(4):
            for k in range(4):
                mid_ref[i * 4 + t, block_of(SLOTS, k), :] = sums[
                    t * 32 : (t + 1) * 32, k * 128 : (k + 1) * 128
                ]
        return carry

    lax.fori_loop(0, 4, chunk, 0)
    count = lax.dot_general(
        onehot(16, slot >> 5), repeated(slot & 31), NT, preferred_element_type=F32
    )
    low, high = split_count(count)
    lane = lax.broadcasted_iota(I32, (1, 512), 1)
    hubs = hub_ref[...].astype(F32)
    which = (onehot(16, lane >> 5).astype(F32) * hubs).astype(BF16)
    hub = lax.dot_general(which, repeated(lane & 31), NT, preferred_element_type=F32)
    row = lax.broadcasted_iota(I32, (8, 128), 0)
    for t in range(16):
        about = jnp.where(row == 0, low[t : t + 1], 0.0)
        about = jnp.where(row == 1, high[t : t + 1], about)
        about = jnp.where(row == 2, hub[t : t + 1], about)
        mid_ref[t, ABOUT:ROWS, :] = about.astype(BF16)


def fill_body(rows_ref, mid_in, mid_ref, wide, block, sems):
    del mid_in
    for z in range(4):
        wide[4 * z : 4 * z + 4, :] = rows_ref[z].astype(F32)
    for k in range(4):
        block[16 * k : 16 * k + 16, :] = wide[:, 128 * k : 128 * k + 128].astype(BF16)
    copies = [
        pltpu.make_async_copy(block, mid_ref.at[t, pl.ds(GATHERED, 64)], sems.at[t])
        for t in range(16)
    ]
    for copy in copies:
        copy.start()
    for copy in copies:
        copy.wait()


def reduce_body(mid_ref, out_hbm, table_ref, out_ref, sem):
    lane = lax.broadcasted_iota(I32, (8, 128), 1)
    blocks = []
    for k in range(4):
        block = jnp.zeros((8, 128), F32)
        for i in range(4):
            block = jnp.where(lane >> 5 == i, mid_ref[4 * k + i, ABOUT:ROWS, :].astype(F32), block)
        blocks.append(block)
    about = jnp.concatenate(blocks, axis=1)
    count = about[0:1] + 256.0 * about[1:2]
    lane = lax.broadcasted_iota(I32, (1, 512), 1)
    target = ((lane & 31) >> 1) * 4 + about[2:3].astype(I32)
    picks = onehot(64, target)
    slots = [mid_ref[:, block_of(SLOTS, k), :].reshape(512, 128) for k in range(4)]
    sums = dot(picks, jnp.concatenate(slots, axis=1))
    degree = jnp.sum(picks.astype(F32) * count, axis=1, keepdims=True)
    low, high = split_count(degree)
    extra_lane = lax.broadcasted_iota(I32, (64, 128), 1)
    extra = jnp.where(extra_lane == 0, low, jnp.where(extra_lane == 1, high, 0.0))
    for g in range(16):
        out_ref[g, :, 0:512] = sums[4 * g : 4 * g + 4].astype(BF16)
        out_ref[g, :, 512:640] = extra[4 * g : 4 * g + 4].astype(BF16)
    copy = pltpu.make_async_copy(out_ref, out_hbm, sem)
    copy.start()
    for k in range(4):
        table_ref[:, 128 * k : 128 * k + 128] = mid_ref[:, block_of(GATHERED, k), :].reshape(256, 128)
    copy.wait()


def counts_body(
    where_ref, src_ref, dst_ref, feats_ref, before_ref, after_ref, hub_ref, weight_ref,
    low_ref, high_ref, degree_ref, hub_linear_ref, partial_ref,
):
    core = where_ref[0]
    side = where_ref[1]
    src = src_ref[...]
    targets = onehot(128, dst_ref[...])
    hub = src - 160
    table = (((hub >> 2) & 1) ^ core) * 2 + (((hub >> 3) & 1) ^ side)
    column = table * 256 + (hub >> 6) * 16 + ((hub >> 2) & 12) + (hub & 3)
    column = jnp.where(hub < 0, -1, column)
    degree_ref[...] = jnp.broadcast_to(
        jnp.sum(targets.astype(F32), axis=1, keepdims=True), degree_ref.shape
    )

    def counted(index, first):
        count = lax.dot_general(
            targets, onehot(256, index, first), NT, preferred_element_type=F32
        )
        low, high = split_count(count)
        return low.astype(BF16), (high * 256.0).astype(BF16)

    def chunk(i, carry):
        low, high = counted(column, i * 256)
        place = pl.ds(pl.multiple_of(i * 256, 256), 256)
        low_ref[:, place] = low
        high_ref[:, place] = high
        return carry

    lax.fori_loop(0, 4, chunk, 0)
    total = jnp.zeros((128, 512), F32)
    for part in counted(src, 0):
        total = total + dot(part[:, 0:128], feats_ref[...])
        total = total + dot(part[:, 128:144], before_ref[...])
        total = total + dot(part[:, 144:160], after_ref[...])
    partial_ref[...] = total
    hub_linear_ref[...] = dot(hub_ref[...], weight_ref[0:512])


def nodes_body(
    low_ref, high_ref, degree_ref, partial_ref, feats_ref,
    table_0, table_1, table_2, table_3, weight_ref, out_ref,
):
    linear = dot(feats_ref[...], weight_ref[0:512])
    total = partial_ref[...]
    for k, table in enumerate((table_0, table_1, table_2, table_3)):
        for ref in (low_ref, high_ref):
            total = total + dot(ref[:, 256 * k : 256 * k + 256], table[...])
    mean = (total / degree_ref[:, 0:1]).astype(BF16)
    out_ref[...] = normalized(linear + dot(mean, weight_ref[512:1024]))


def hubs_body(parts_ref, linear_ref, weight_ref, out_ref):
    total = jnp.zeros((4, 640), F32)
    for g in range(16):
        total = total + parts_ref[g].astype(F32)
    degree = total[:, 512:513] + 256.0 * total[:, 513:514]
    mean = (total[:, 0:512] / degree).astype(BF16)
    out_ref[...] = normalized(linear_ref[...] + dot(mean, weight_ref[512:1024]))


VMEM = pl.BlockSpec(memory_space=pltpu.VMEM)
SMEM = pl.BlockSpec(memory_space=pltpu.SMEM)
ANY = pl.BlockSpec(memory_space=pl.ANY)
HBM = pl.BlockSpec(memory_space=pltpu.HBM)


def call(body, out, specs, flops, nbytes, limit=16, **more):
    out_specs = more.pop("out_specs", jax.tree.map(lambda _: VMEM, out))
    return pl.pallas_call(
        body,
        out_shape=out,
        in_specs=specs,
        out_specs=out_specs,
        compiler_params=pltpu.CompilerParams(vmem_limit_bytes=limit * MIB),
        cost_estimate=pl.CostEstimate(flops=flops, bytes_accessed=nbytes, transcendentals=0),
        **more,
    )


def shape(*dims, dtype=BF16):
    return jax.ShapeDtypeStruct(dims, dtype)


def in_hbm(*arrays):
    return [pltpu.with_memory_space_constraint(a, pltpu.HBM) for a in arrays]


def on_device(
    node_feats, hub_feats, weight, edge_src, edge_dst, bound_rows,
    hub_edge_src, hub_edge_slot, slot_hub,
):
    where = jnp.stack([lax.axis_index("core"), lax.axis_index("side")]).astype(I32)
    gathered = lax.all_to_all(
        jnp.broadcast_to(hub_feats[None], (4, 4, 512)), "pair", 0, 0, tiled=True
    )
    mid = call(
        slots_body, shape(16, ROWS, 128), [HBM] * 4, 1 << 30, 2 << 20,
        scratch_shapes=[
            pltpu.VMEM((1, 1024), I32),
            pltpu.VMEM((1, 1024), I32),
            pltpu.VMEM((1, 512), I32),
            pltpu.VMEM((128, 512), BF16),
            pltpu.SemaphoreType.DMA((4,)),
        ],
    )(*in_hbm(hub_edge_src, hub_edge_slot, slot_hub, node_feats))
    mid = call(
        fill_body, shape(16, ROWS, 128), [VMEM, ANY], 0, 1 << 20,
        out_specs=ANY,
        input_output_aliases={1: 0},
        scratch_shapes=[
            pltpu.VMEM((16, 512), F32),
            pltpu.VMEM((64, 128), BF16),
            pltpu.SemaphoreType.DMA((16,)),
        ],
    )(gathered, mid)
    mid = lax.all_to_all(mid, OUTER, 0, 0, tiled=True)
    exports = call(export_body, shape(16, 512), [VMEM] * 2, 2 << 20, 150000)(bound_rows, node_feats)
    count = lax.axis_size(DOM)
    forward = [(i, (i + 1) % count) for i in range(count)]
    backward = [(target, source) for source, target in forward]
    before = lax.ppermute(exports, DOM, forward)
    after = lax.ppermute(exports, DOM, backward)
    low, high, degree, hub_linear, partial = call(
        counts_body,
        (
            shape(128, 1024), shape(128, 1024), shape(128, 128, dtype=F32),
            shape(4, 512, dtype=F32), shape(128, 512, dtype=F32),
        ),
        [SMEM] + [VMEM] * 7, 1 << 30, 2 << 20,
    )(where, edge_src, edge_dst, node_feats, before, after, hub_feats, weight)
    parts, table_0 = call(
        reduce_body, (pltpu.HBM((16, 4, 640), BF16), shape(256, 512)), [VMEM],
        1 << 26, 2 << 20,
        out_specs=(HBM, VMEM),
        scratch_shapes=[pltpu.VMEM((16, 4, 640), BF16), pltpu.SemaphoreType.DMA],
    )(mid)
    swap = [(0, 1), (1, 0)]
    table_1 = lax.ppermute(table_0, "side", swap)
    parts = lax.all_to_all(parts, INNER, 0, 0, tiled=True)
    table_2 = lax.ppermute(table_0, "core", swap)
    table_3 = lax.ppermute(table_1, "core", swap)
    node_out = call(nodes_body, shape(128, 512), [VMEM] * 10, 1 << 29, 2 << 20)(
        low, high, degree, partial, node_feats, table_0, table_1, table_2, table_3, weight
    )
    hub_out = call(hubs_body, shape(4, 512), [VMEM] * 3, 1 << 22, 1 << 19)(
        parts, hub_linear, weight
    )
    return (node_out, hub_out)


def solution(mesh):
    finer = Mesh(mesh.devices.reshape(4, 4, 4, 2, 2), ROLE_DOM)
    rows = P(ROLE_DOM, None)
    in_specs = (rows, rows, P(), rows, rows, rows, rows, rows, rows)
    return jax.shard_map(
        on_device, mesh=finer, in_specs=in_specs, out_specs=(rows, rows), check_vma=False
    )
```

```python
import jax
import jax.numpy as jnp
from jax import lax
from jax.experimental import pallas as pl
from jax.experimental.pallas import tpu as pltpu
from jax.sharding import Mesh
from jax.sharding import PartitionSpec as P


INNER = ("pair", "side", "core")
OUTER = ("role", "x")
DOM = ("x", "pair", "side", "core")
ROLE_DOM = ("role", "x", "pair", "side", "core")

epsilon = 1e-06
F32 = jnp.float32
BF16 = jnp.bfloat16
I32 = jnp.int32
NT = (((1,), (1,)), ((), ()))
TN = (((0,), (0,)), ((), ()))
MIB = 1 << 20


def dot(a, b):
    return jnp.dot(a, b, preferred_element_type=F32)


def onehot(rows, index, first=0):
    shape = (rows, index.shape[1])
    return jnp.where(lax.broadcasted_iota(I32, shape, 0) + first == index, 1.0, 0.0).astype(BF16)


def split_count(count):
    high = jnp.floor(count * (1.0 / 256.0))
    return count - high * 256.0, high


def normalized(linear):
    rectified = jnp.maximum(linear, 0.0)
    mean = jnp.mean(rectified * rectified, axis=1, keepdims=True)
    return (rectified * lax.rsqrt(mean + epsilon)).astype(BF16)


def export_body(bound_ref, feats_ref, out_ref):
    picks = onehot(feats_ref.shape[0], bound_ref[...])
    out_ref[...] = lax.dot_general(picks, feats_ref[...], TN, preferred_element_type=F32).astype(BF16)


def repeated(index):
    shape = (128, index.shape[1])
    row = lax.broadcasted_iota(I32, shape, 0) & 31
    return jnp.where(row == index, 1.0, 0.0).astype(BF16)


GATHERED, SLOTS, ABOUT, ROWS = 0, 64, 192, 200


def block_of(first, k):
    size = (SLOTS if first == GATHERED else ABOUT - SLOTS) // 4
    return pl.ds(first + size * k, size)


def slots_body(
    src_hbm, slot_hbm, hub_hbm, feats_hbm, mid_hbm,
    src_ref, slot_ref, hub_ref, feats_ref, sems, mid_ref, out_sems,
):
    copies = [
        pltpu.make_async_copy(source, target, sems.at[k])
        for k, (source, target) in enumerate(
            ((src_hbm, src_ref), (slot_hbm, slot_ref), (hub_hbm, hub_ref), (feats_hbm, feats_ref))
        )
    ]
    for copy in copies:
        copy.start()
    for copy in copies:
        copy.wait()
    feats = feats_ref[...]
    slot = slot_ref[...]
    picks = onehot(128, src_ref[...])
    count = lax.dot_general(
        onehot(16, slot >> 5), repeated(slot & 31), NT, preferred_element_type=F32
    )
    low, high = split_count(count)
    lane = lax.broadcasted_iota(I32, (1, 512), 1)
    hubs = hub_ref[...].astype(F32)
    which = (onehot(16, lane >> 5).astype(F32) * hubs).astype(BF16)
    hub = lax.dot_general(which, repeated(lane & 31), NT, preferred_element_type=F32)
    row = lax.broadcasted_iota(I32, (8, 128), 0)
    for t in range(16):
        about = jnp.where(row == 0, low[t : t + 1], 0.0)
        about = jnp.where(row == 1, high[t : t + 1], about)
        about = jnp.where(row == 2, hub[t : t + 1], about)
        mid_ref[t, ABOUT - SLOTS : ROWS - SLOTS, :] = about.astype(BF16)
    copies = []
    for i in range(4):
        count = lax.dot_general(
            onehot(128, slot, i * 128), picks, NT, preferred_element_type=F32
        )
        low, high = split_count(count)
        sums = dot(low.astype(BF16), feats) + dot((high * 256.0).astype(BF16), feats)
        sums = sums.astype(BF16)
        for t in range(4):
            for k in range(4):
                mid_ref[i * 4 + t, 32 * k : 32 * k + 32, :] = sums[
                    t * 32 : (t + 1) * 32, k * 128 : (k + 1) * 128
                ]
        copies.append(
            pltpu.make_async_copy(
                mid_ref.at[pl.ds(4 * i, 4)],
                mid_hbm.at[pl.ds(4 * i, 4), pl.ds(SLOTS, ROWS - SLOTS)],
                out_sems.at[i],
            )
        )
        copies[-1].start()
    for copy in copies:
        copy.wait()


def fill_body(rows_0, rows_1, rows_2, rows_3, mid_in, mid_ref, wide, block, sems):
    del mid_in
    for k, rows in enumerate((rows_0, rows_1, rows_2, rows_3)):
        wide[4 * k : 4 * k + 4, :] = rows[...].astype(F32)
    for k in range(4):
        block[16 * k : 16 * k + 16, :] = wide[:, 128 * k : 128 * k + 128].astype(BF16)
    copies = [
        pltpu.make_async_copy(block, mid_ref.at[t, pl.ds(GATHERED, 64)], sems.at[t])
        for t in range(16)
    ]
    for copy in copies:
        copy.start()
    for copy in copies:
        copy.wait()


def reduce_body(mid_ref, out_hbm, table_ref, out_ref, sem):
    lane = lax.broadcasted_iota(I32, (8, 128), 1)
    blocks = []
    for k in range(4):
        block = jnp.zeros((8, 128), F32)
        for i in range(4):
            block = jnp.where(lane >> 5 == i, mid_ref[4 * k + i, ABOUT:ROWS, :].astype(F32), block)
        blocks.append(block)
    about = jnp.concatenate(blocks, axis=1)
    count = about[0:1] + 256.0 * about[1:2]
    lane = lax.broadcasted_iota(I32, (1, 512), 1)
    target = ((lane & 31) >> 1) * 4 + about[2:3].astype(I32)
    picks = onehot(64, target)
    slots = [mid_ref[:, block_of(SLOTS, k), :].reshape(512, 128) for k in range(4)]
    sums = dot(picks, jnp.concatenate(slots, axis=1))
    degree = jnp.sum(picks.astype(F32) * count, axis=1, keepdims=True)
    low, high = split_count(degree)
    extra_lane = lax.broadcasted_iota(I32, (64, 128), 1)
    extra = jnp.where(extra_lane == 0, low, jnp.where(extra_lane == 1, high, 0.0))
    for g in range(16):
        out_ref[g, :, 0:512] = sums[4 * g : 4 * g + 4].astype(BF16)
        out_ref[g, :, 512:640] = extra[4 * g : 4 * g + 4].astype(BF16)
    copy = pltpu.make_async_copy(out_ref, out_hbm, sem)
    copy.start()
    for k in range(4):
        table_ref[:, 128 * k : 128 * k + 128] = mid_ref[:, block_of(GATHERED, k), :].reshape(256, 128)
    copy.wait()


def counts_body(
    where_ref, src_ref, dst_ref, feats_ref, hub_ref, weight_ref,
    low_ref, high_ref, degree_ref, hub_linear_ref, partial_ref,
):
    core = where_ref[0]
    side = where_ref[1]
    pair = where_ref[2]
    src = src_ref[...]
    targets = onehot(128, dst_ref[...])
    hub = src - 160
    table = (((hub >> 2) & 1) ^ core) * 2 + (((hub >> 3) & 1) ^ side)
    column = table * 256 + (hub >> 6) * 16 + (((hub >> 4) - pair) & 3) * 4 + (hub & 3)
    column = jnp.where(hub < 0, -1, column)
    degree_ref[...] = jnp.broadcast_to(
        jnp.sum(targets.astype(F32), axis=1, keepdims=True), degree_ref.shape
    )

    def counted(index, first):
        count = lax.dot_general(
            targets, onehot(256, index, first), NT, preferred_element_type=F32
        )
        low, high = split_count(count)
        return low.astype(BF16), (high * 256.0).astype(BF16)

    def chunk(i, carry):
        low, high = counted(column, i * 256)
        place = pl.ds(pl.multiple_of(i * 256, 256), 256)
        low_ref[:, place] = low
        high_ref[:, place] = high
        return carry

    lax.fori_loop(0, 4, chunk, 0)
    total = jnp.zeros((128, 512), F32)
    for part, ref in zip(counted(src, 0), (low_ref, high_ref)):
        total = total + dot(part[:, 0:128], feats_ref[...])
        ref[:, 1024:1152] = part[:, 128:256]
    partial_ref[...] = total
    hub_linear_ref[...] = dot(hub_ref[...], weight_ref[0:512])


def nodes_body(
    low_ref, high_ref, partial_ref, feats_ref, before_ref, after_ref, table_0, table_1, weight_ref,
    total_ref, linear_ref,
):
    linear_ref[...] = dot(feats_ref[...], weight_ref[0:512])
    total = partial_ref[...]
    for ref in (low_ref, high_ref):
        total = total + dot(ref[:, 1024:1040], before_ref[...])
        total = total + dot(ref[:, 1040:1056], after_ref[...])
        total = total + dot(ref[:, 0:256], table_0[...]) + dot(ref[:, 256:512], table_1[...])
    total_ref[...] = total


def finish_body(
    low_ref, high_ref, degree_ref, total_ref, linear_ref, table_2, table_3, weight_ref, out_ref
):
    total = total_ref[...]
    for ref in (low_ref, high_ref):
        total = total + dot(ref[:, 512:768], table_2[...]) + dot(ref[:, 768:1024], table_3[...])
    mean = (total / degree_ref[:, 0:1]).astype(BF16)
    out_ref[...] = normalized(linear_ref[...] + dot(mean, weight_ref[512:1024]))


def hubs_body(parts_ref, linear_ref, weight_ref, out_ref):
    total = jnp.zeros((4, 640), F32)
    for g in range(16):
        total = total + parts_ref[g].astype(F32)
    degree = total[:, 512:513] + 256.0 * total[:, 513:514]
    mean = (total[:, 0:512] / degree).astype(BF16)
    out_ref[...] = normalized(linear_ref[...] + dot(mean, weight_ref[512:1024]))


VMEM = pl.BlockSpec(memory_space=pltpu.VMEM)
SMEM = pl.BlockSpec(memory_space=pltpu.SMEM)
ANY = pl.BlockSpec(memory_space=pl.ANY)
HBM = pl.BlockSpec(memory_space=pltpu.HBM)


def call(body, out, specs, flops, nbytes, limit=16, **more):
    out_specs = more.pop("out_specs", jax.tree.map(lambda _: VMEM, out))
    return pl.pallas_call(
        body,
        out_shape=out,
        in_specs=specs,
        out_specs=out_specs,
        compiler_params=pltpu.CompilerParams(vmem_limit_bytes=limit * MIB),
        cost_estimate=pl.CostEstimate(flops=flops, bytes_accessed=nbytes, transcendentals=0),
        **more,
    )


def shape(*dims, dtype=BF16):
    return jax.ShapeDtypeStruct(dims, dtype)


def in_hbm(*arrays):
    return [pltpu.with_memory_space_constraint(a, pltpu.HBM) for a in arrays]


def on_device(
    node_feats, hub_feats, weight, edge_src, edge_dst, bound_rows,
    hub_edge_src, hub_edge_slot, slot_hub,
):
    axes = ("core", "side", "pair")
    where = jnp.stack([lax.axis_index(axis) for axis in axes]).astype(I32)
    pairs = lax.axis_size("pair")
    gathered = []
    for k in (1, 2, 3):
        ring = [(i, (i - k) % pairs) for i in range(pairs)]
        gathered.append(lax.ppermute(hub_feats, "pair", ring))
    mid = call(
        slots_body, pltpu.HBM((16, ROWS, 128), BF16), [HBM] * 4, 1 << 30, 2 << 20,
        out_specs=HBM,
        scratch_shapes=[
            pltpu.VMEM((1, 1024), I32),
            pltpu.VMEM((1, 1024), I32),
            pltpu.VMEM((1, 512), I32),
            pltpu.VMEM((128, 512), BF16),
            pltpu.SemaphoreType.DMA((4,)),
            pltpu.VMEM((16, ROWS - SLOTS, 128), BF16),
            pltpu.SemaphoreType.DMA((4,)),
        ],
    )(*in_hbm(hub_edge_src, hub_edge_slot, slot_hub, node_feats))
    mid = call(
        fill_body, pltpu.HBM((16, ROWS, 128), BF16), [VMEM] * 4 + [HBM], 0, 1 << 20,
        out_specs=HBM,
        input_output_aliases={4: 0},
        scratch_shapes=[
            pltpu.VMEM((16, 512), F32),
            pltpu.VMEM((64, 128), BF16),
            pltpu.SemaphoreType.DMA((16,)),
        ],
    )(hub_feats, *gathered, mid)
    mid = lax.all_to_all(mid, OUTER, 0, 0, tiled=True)
    exports = call(export_body, shape(16, 512), [VMEM] * 2, 2 << 20, 150000)(bound_rows, node_feats)
    count = lax.axis_size(DOM)
    forward = [(i, (i + 1) % count) for i in range(count)]
    backward = [(target, source) for source, target in forward]
    before = lax.ppermute(exports, DOM, forward)
    after = lax.ppermute(exports, DOM, backward)
    low, high, degree, hub_linear, partial = call(
        counts_body,
        (
            shape(128, 1152), shape(128, 1152), shape(128, 128, dtype=F32),
            shape(4, 512, dtype=F32), shape(128, 512, dtype=F32),
        ),
        [SMEM] + [VMEM] * 5, 1 << 30, 2 << 20,
    )(where, edge_src, edge_dst, node_feats, hub_feats, weight)
    parts, table_0 = call(
        reduce_body, (pltpu.HBM((16, 4, 640), BF16), shape(256, 512)), [VMEM],
        1 << 26, 2 << 20,
        out_specs=(HBM, VMEM),
        scratch_shapes=[pltpu.VMEM((16, 4, 640), BF16), pltpu.SemaphoreType.DMA],
    )(mid)
    swap = [(0, 1), (1, 0)]
    table_1 = lax.ppermute(table_0, "side", swap)
    parts = lax.all_to_all(parts, INNER, 0, 0, tiled=True)
    table_2 = lax.ppermute(table_0, "core", swap)
    table_3 = lax.ppermute(table_1, "core", swap)
    wide = shape(128, 512, dtype=F32)
    total, linear = call(nodes_body, (wide, wide), [VMEM] * 9, 1 << 28, 1 << 20)(
        low, high, partial, node_feats, before, after, table_0, table_1, weight
    )
    node_out = call(finish_body, shape(128, 512), [VMEM] * 8, 1 << 28, 1 << 20)(
        low, high, degree, total, linear, table_2, table_3, weight
    )
    hub_out = call(hubs_body, shape(4, 512), [VMEM] * 3, 1 << 22, 1 << 19)(
        parts, hub_linear, weight
    )
    return (node_out, hub_out)


def solution(mesh):
    finer = Mesh(mesh.devices.reshape(4, 4, 4, 2, 2), ROLE_DOM)
    rows = P(ROLE_DOM, None)
    in_specs = (rows, rows, P(), rows, rows, rows, rows, rows, rows)
    return jax.shard_map(
        on_device, mesh=finer, in_specs=in_specs, out_specs=(rows, rows), check_vma=False
    )
```

```python
import jax
import jax.numpy as jnp
from jax import lax
from jax.experimental import pallas as pl
from jax.experimental.pallas import tpu as pltpu
from jax.sharding import Mesh
from jax.sharding import PartitionSpec as P


INNER = ("far", "near", "side", "core")
OUTER = ("role", "x")
DOM = ("x", "far", "near", "side", "core")
ROLE_DOM = ("role", "x", "far", "near", "side", "core")

epsilon = 1e-06
F32 = jnp.float32
BF16 = jnp.bfloat16
I32 = jnp.int32
NT = (((1,), (1,)), ((), ()))
TN = (((0,), (0,)), ((), ()))
MIB = 1 << 20


def dot(a, b):
    return jnp.dot(a, b, preferred_element_type=F32)


def onehot(rows, index, first=0):
    shape = (rows, index.shape[1])
    return jnp.where(lax.broadcasted_iota(I32, shape, 0) + first == index, 1.0, 0.0).astype(BF16)


def split_count(count):
    high = jnp.floor(count * (1.0 / 256.0))
    return count - high * 256.0, high


def normalized(linear):
    rectified = jnp.maximum(linear, 0.0)
    mean = jnp.mean(rectified * rectified, axis=1, keepdims=True)
    return (rectified * lax.rsqrt(mean + epsilon)).astype(BF16)


def export_body(bound_ref, feats_ref, out_ref):
    picks = onehot(feats_ref.shape[0], bound_ref[...])
    out_ref[...] = lax.dot_general(picks, feats_ref[...], TN, preferred_element_type=F32).astype(BF16)


def repeated(index):
    shape = (128, index.shape[1])
    row = lax.broadcasted_iota(I32, shape, 0) & 31
    return jnp.where(row == index, 1.0, 0.0).astype(BF16)


GATHERED, SLOTS, ABOUT, ROWS = 0, 32, 160, 168


def block_of(first, k):
    size = (SLOTS if first == GATHERED else ABOUT - SLOTS) // 4
    return pl.ds(first + size * k, size)


def slots_body(
    src_hbm, slot_hbm, hub_hbm, feats_hbm, mid_hbm,
    src_ref, slot_ref, hub_ref, feats_ref, sems, mid_ref, out_sems,
):
    copies = [
        pltpu.make_async_copy(source, target, sems.at[k])
        for k, (source, target) in enumerate(
            ((src_hbm, src_ref), (slot_hbm, slot_ref), (hub_hbm, hub_ref), (feats_hbm, feats_ref))
        )
    ]
    for copy in copies:
        copy.start()
    for copy in copies:
        copy.wait()
    feats = feats_ref[...]
    slot = slot_ref[...]
    picks = onehot(128, src_ref[...])
    count = lax.dot_general(
        onehot(16, slot >> 5), repeated(slot & 31), NT, preferred_element_type=F32
    )
    low, high = split_count(count)
    lane = lax.broadcasted_iota(I32, (1, 512), 1)
    hubs = hub_ref[...].astype(F32)
    which = (onehot(16, lane >> 5).astype(F32) * hubs).astype(BF16)
    hub = lax.dot_general(which, repeated(lane & 31), NT, preferred_element_type=F32)
    row = lax.broadcasted_iota(I32, (8, 128), 0)
    for t in range(16):
        about = jnp.where(row == 0, low[t : t + 1], 0.0)
        about = jnp.where(row == 1, high[t : t + 1], about)
        about = jnp.where(row == 2, hub[t : t + 1], about)
        mid_ref[t, ABOUT - SLOTS : ROWS - SLOTS, :] = about.astype(BF16)
    copies = []
    for i in range(4):
        count = lax.dot_general(
            onehot(128, slot, i * 128), picks, NT, preferred_element_type=F32
        )
        low, high = split_count(count)
        sums = dot(low.astype(BF16), feats) + dot((high * 256.0).astype(BF16), feats)
        sums = sums.astype(BF16)
        for t in range(4):
            for k in range(4):
                mid_ref[i * 4 + t, 32 * k : 32 * k + 32, :] = sums[
                    t * 32 : (t + 1) * 32, k * 128 : (k + 1) * 128
                ]
        copies.append(
            pltpu.make_async_copy(
                mid_ref.at[pl.ds(4 * i, 4)],
                mid_hbm.at[pl.ds(4 * i, 4), pl.ds(SLOTS, ROWS - SLOTS)],
                out_sems.at[i],
            )
        )
        copies[-1].start()
    for copy in copies:
        copy.wait()


def fill_body(rows_0, rows_1, mid_in, mid_ref, wide, block, sems):
    del mid_in
    for k, rows in enumerate((rows_0, rows_1)):
        wide[4 * k : 4 * k + 4, :] = rows[...].astype(F32)
    for k in range(4):
        block[8 * k : 8 * k + 8, :] = wide[:, 128 * k : 128 * k + 128].astype(BF16)
    copies = [
        pltpu.make_async_copy(block, mid_ref.at[t, pl.ds(GATHERED, 32)], sems.at[t])
        for t in range(16)
    ]
    for copy in copies:
        copy.start()
    for copy in copies:
        copy.wait()


def reduce_body(mid_ref, out_hbm, table_ref, out_ref, sem):
    lane = lax.broadcasted_iota(I32, (8, 128), 1)
    blocks = []
    for k in range(4):
        block = jnp.zeros((8, 128), F32)
        for i in range(4):
            block = jnp.where(lane >> 5 == i, mid_ref[4 * k + i, ABOUT:ROWS, :].astype(F32), block)
        blocks.append(block)
    about = jnp.concatenate(blocks, axis=1)
    count = about[0:1] + 256.0 * about[1:2]
    lane = lax.broadcasted_iota(I32, (1, 512), 1)
    target = ((lane & 31) >> 1) * 4 + about[2:3].astype(I32)
    picks = onehot(64, target)
    slots = [mid_ref[:, block_of(SLOTS, k), :].reshape(512, 128) for k in range(4)]
    sums = dot(picks, jnp.concatenate(slots, axis=1))
    degree = jnp.sum(picks.astype(F32) * count, axis=1, keepdims=True)
    low, high = split_count(degree)
    extra_lane = lax.broadcasted_iota(I32, (64, 128), 1)
    extra = jnp.where(extra_lane == 0, low, jnp.where(extra_lane == 1, high, 0.0))
    for g in range(16):
        out_ref[g, :, 0:512] = sums[4 * g : 4 * g + 4].astype(BF16)
        out_ref[g, :, 512:640] = extra[4 * g : 4 * g + 4].astype(BF16)
    copy = pltpu.make_async_copy(out_ref, out_hbm, sem)
    copy.start()
    for k in range(4):
        table_ref[:, 128 * k : 128 * k + 128] = mid_ref[:, block_of(GATHERED, k), :].reshape(128, 128)
    copy.wait()


def counts_body(
    where_ref, src_ref, dst_ref, feats_ref, hub_ref, weight_ref,
    low_ref, high_ref, degree_ref, hub_linear_ref, partial_ref,
):
    core = where_ref[0]
    side = where_ref[1]
    near = where_ref[2]
    far = where_ref[3]
    src = src_ref[...]
    targets = onehot(128, dst_ref[...])
    hub = src - 160
    table = (((hub >> 2) & 1) ^ core) * 4 + (((hub >> 4) & 1) ^ near) * 2 + (((hub >> 3) & 1) ^ side)
    column = table * 128 + (hub >> 6) * 8 + (((hub >> 5) & 1) ^ far) * 4 + (hub & 3)
    column = jnp.where(hub < 0, -1, column)
    degree_ref[...] = jnp.broadcast_to(
        jnp.sum(targets.astype(F32), axis=1, keepdims=True), degree_ref.shape
    )

    def counted(index, first):
        count = lax.dot_general(
            targets, onehot(256, index, first), NT, preferred_element_type=F32
        )
        low, high = split_count(count)
        return low.astype(BF16), (high * 256.0).astype(BF16)

    def chunk(i, carry):
        low, high = counted(column, i * 256)
        place = pl.ds(pl.multiple_of(i * 256, 256), 256)
        low_ref[:, place] = low
        high_ref[:, place] = high
        return carry

    lax.fori_loop(0, 4, chunk, 0)
    total = jnp.zeros((128, 512), F32)
    for part, ref in zip(counted(src, 0), (low_ref, high_ref)):
        total = total + dot(part[:, 0:128], feats_ref[...])
        ref[:, 1024:1152] = part[:, 128:256]
    partial_ref[...] = total
    hub_linear_ref[...] = dot(hub_ref[...], weight_ref[0:512])


def nodes_body(
    low_ref, high_ref, partial_ref, feats_ref, before_ref, after_ref,
    table_0, table_1, table_2, table_3, weight_ref,
    total_ref, linear_ref,
):
    linear_ref[...] = dot(feats_ref[...], weight_ref[0:512])
    total = partial_ref[...]
    tables = jnp.concatenate([t[...] for t in (table_0, table_1, table_2, table_3)], axis=0)
    for ref in (low_ref, high_ref):
        total = total + dot(ref[:, 1024:1040], before_ref[...])
        total = total + dot(ref[:, 1040:1056], after_ref[...])
        total = total + dot(ref[:, 0:512], tables)
    total_ref[...] = total


def finish_body(
    low_ref, high_ref, degree_ref, total_ref, linear_ref,
    table_4, table_5, table_6, table_7, weight_ref, out_ref,
):
    total = total_ref[...]
    tables = jnp.concatenate([t[...] for t in (table_4, table_5, table_6, table_7)], axis=0)
    for ref in (low_ref, high_ref):
        total = total + dot(ref[:, 512:1024], tables)
    mean = (total / degree_ref[:, 0:1]).astype(BF16)
    out_ref[...] = normalized(linear_ref[...] + dot(mean, weight_ref[512:1024]))


def hubs_body(parts_ref, linear_ref, weight_ref, out_ref):
    total = jnp.zeros((4, 640), F32)
    for g in range(16):
        total = total + parts_ref[g].astype(F32)
    degree = total[:, 512:513] + 256.0 * total[:, 513:514]
    mean = (total[:, 0:512] / degree).astype(BF16)
    out_ref[...] = normalized(linear_ref[...] + dot(mean, weight_ref[512:1024]))


VMEM = pl.BlockSpec(memory_space=pltpu.VMEM)
SMEM = pl.BlockSpec(memory_space=pltpu.SMEM)
ANY = pl.BlockSpec(memory_space=pl.ANY)
HBM = pl.BlockSpec(memory_space=pltpu.HBM)


def call(body, out, specs, flops, nbytes, limit=16, **more):
    out_specs = more.pop("out_specs", jax.tree.map(lambda _: VMEM, out))
    return pl.pallas_call(
        body,
        out_shape=out,
        in_specs=specs,
        out_specs=out_specs,
        compiler_params=pltpu.CompilerParams(vmem_limit_bytes=limit * MIB),
        cost_estimate=pl.CostEstimate(flops=flops, bytes_accessed=nbytes, transcendentals=0),
        **more,
    )


def shape(*dims, dtype=BF16):
    return jax.ShapeDtypeStruct(dims, dtype)


def in_hbm(*arrays):
    return [pltpu.with_memory_space_constraint(a, pltpu.HBM) for a in arrays]


def on_device(
    node_feats, hub_feats, weight, edge_src, edge_dst, bound_rows,
    hub_edge_src, hub_edge_slot, slot_hub,
):
    axes = ("core", "side", "near", "far")
    where = jnp.stack([lax.axis_index(axis) for axis in axes]).astype(I32)
    swap = [(0, 1), (1, 0)]
    gathered = lax.ppermute(hub_feats, "far", swap)
    mid = call(
        slots_body, pltpu.HBM((16, ROWS, 128), BF16), [HBM] * 4, 1 << 30, 2 << 20,
        out_specs=HBM,
        scratch_shapes=[
            pltpu.VMEM((1, 1024), I32),
            pltpu.VMEM((1, 1024), I32),
            pltpu.VMEM((1, 512), I32),
            pltpu.VMEM((128, 512), BF16),
            pltpu.SemaphoreType.DMA((4,)),
            pltpu.VMEM((16, ROWS - SLOTS, 128), BF16),
            pltpu.SemaphoreType.DMA((4,)),
        ],
    )(*in_hbm(hub_edge_src, hub_edge_slot, slot_hub, node_feats))
    mid = call(
        fill_body, pltpu.HBM((16, ROWS, 128), BF16), [VMEM] * 2 + [HBM], 0, 1 << 20,
        out_specs=HBM,
        input_output_aliases={2: 0},
        scratch_shapes=[
            pltpu.VMEM((8, 512), F32),
            pltpu.VMEM((32, 128), BF16),
            pltpu.SemaphoreType.DMA((16,)),
        ],
    )(hub_feats, gathered, mid)
    mid = lax.all_to_all(mid, OUTER, 0, 0, tiled=True)
    exports = call(export_body, shape(16, 512), [VMEM] * 2, 2 << 20, 150000)(bound_rows, node_feats)
    count = lax.axis_size(DOM)
    forward = [(i, (i + 1) % count) for i in range(count)]
    backward = [(target, source) for source, target in forward]
    before = lax.ppermute(exports, DOM, forward)
    after = lax.ppermute(exports, DOM, backward)
    low, high, degree, hub_linear, partial = call(
        counts_body,
        (
            shape(128, 1152), shape(128, 1152), shape(128, 128, dtype=F32),
            shape(4, 512, dtype=F32), shape(128, 512, dtype=F32),
        ),
        [SMEM] + [VMEM] * 5, 1 << 30, 2 << 20,
    )(where, edge_src, edge_dst, node_feats, hub_feats, weight)
    parts, table_0 = call(
        reduce_body, (pltpu.HBM((16, 4, 640), BF16), shape(128, 512)), [VMEM],
        1 << 26, 2 << 20,
        out_specs=(HBM, VMEM),
        scratch_shapes=[pltpu.VMEM((16, 4, 640), BF16), pltpu.SemaphoreType.DMA],
    )(mid)
    table_1 = lax.ppermute(table_0, "side", swap)
    table_2 = lax.ppermute(table_0, "near", swap)
    table_3 = lax.ppermute(table_0, ("near", "side"), [(i, i ^ 3) for i in range(4)])
    parts = lax.all_to_all(parts, INNER, 0, 0, tiled=True)
    tables = [table_0, table_1, table_2, table_3]
    others = []
    for table in tables:
        others.append(lax.ppermute(table, "core", swap))
    wide = shape(128, 512, dtype=F32)
    total, linear = call(nodes_body, (wide, wide), [VMEM] * 11, 1 << 28, 1 << 20)(
        low, high, partial, node_feats, before, after, *tables, weight
    )
    node_out = call(finish_body, shape(128, 512), [VMEM] * 10, 1 << 28, 1 << 20)(
        low, high, degree, total, linear, *others, weight
    )
    hub_out = call(hubs_body, shape(4, 512), [VMEM] * 3, 1 << 22, 1 << 19)(
        parts, hub_linear, weight
    )
    return (node_out, hub_out)


def solution(mesh):
    finer = Mesh(mesh.devices.reshape(4, 4, 2, 2, 2, 2), ROLE_DOM)
    rows = P(ROLE_DOM, None)
    in_specs = (rows, rows, P(), rows, rows, rows, rows, rows, rows)
    return jax.shard_map(
        on_device, mesh=finer, in_specs=in_specs, out_specs=(rows, rows), check_vma=False
    )
```

```python
import jax
import jax.numpy as jnp
from jax import lax
from jax.experimental import pallas as pl
from jax.experimental.pallas import tpu as pltpu
from jax.sharding import Mesh
from jax.sharding import PartitionSpec as P


INNER = ("far", "near", "side", "core")
OUTER = ("role", "x")
DOM = ("x", "far", "near", "side", "core")
ROLE_DOM = ("role", "x", "far", "near", "side", "core")

epsilon = 1e-06
F32 = jnp.float32
BF16 = jnp.bfloat16
I32 = jnp.int32
NT = (((1,), (1,)), ((), ()))
TN = (((0,), (0,)), ((), ()))
MIB = 1 << 20


def dot(a, b):
    return jnp.dot(a, b, preferred_element_type=F32)


def onehot(rows, index, first=0):
    shape = (rows, index.shape[1])
    return jnp.where(lax.broadcasted_iota(I32, shape, 0) + first == index, 1.0, 0.0).astype(BF16)


def split_count(count):
    high = jnp.floor(count * (1.0 / 256.0))
    return count - high * 256.0, high


def normalized(linear):
    rectified = jnp.maximum(linear, 0.0)
    mean = jnp.mean(rectified * rectified, axis=1, keepdims=True)
    return (rectified * lax.rsqrt(mean + epsilon)).astype(BF16)


def export_body(bound_ref, feats_ref, out_ref):
    picks = onehot(feats_ref.shape[0], bound_ref[...])
    out_ref[...] = lax.dot_general(picks, feats_ref[...], TN, preferred_element_type=F32).astype(BF16)


def repeated(index):
    shape = (128, index.shape[1])
    row = lax.broadcasted_iota(I32, shape, 0) & 31
    return jnp.where(row == index, 1.0, 0.0).astype(BF16)


GATHERED, SLOTS, ABOUT, ROWS = 0, 32, 160, 168


def block_of(first, k):
    size = (SLOTS if first == GATHERED else ABOUT - SLOTS) // 4
    return pl.ds(first + size * k, size)


def slots_body(
    src_hbm, slot_hbm, hub_hbm, feats_hbm, mid_hbm,
    src_ref, slot_ref, hub_ref, feats_ref, sems, mid_ref, out_sems,
):
    copies = [
        pltpu.make_async_copy(source, target, sems.at[k])
        for k, (source, target) in enumerate(
            ((src_hbm, src_ref), (slot_hbm, slot_ref), (hub_hbm, hub_ref), (feats_hbm, feats_ref))
        )
    ]
    for copy in copies:
        copy.start()
    for copy in copies:
        copy.wait()
    feats = feats_ref[...]
    slot = slot_ref[...]
    picks = onehot(128, src_ref[...])
    count = lax.dot_general(
        onehot(16, slot >> 5), repeated(slot & 31), NT, preferred_element_type=F32
    )
    low, high = split_count(count)
    lane = lax.broadcasted_iota(I32, (1, 512), 1)
    hubs = hub_ref[...].astype(F32)
    which = (onehot(16, lane >> 5).astype(F32) * hubs).astype(BF16)
    hub = lax.dot_general(which, repeated(lane & 31), NT, preferred_element_type=F32)
    row = lax.broadcasted_iota(I32, (8, 128), 0)
    for t in range(16):
        about = jnp.where(row == 0, low[t : t + 1], 0.0)
        about = jnp.where(row == 1, high[t : t + 1], about)
        about = jnp.where(row == 2, hub[t : t + 1], about)
        mid_ref[t, ABOUT - SLOTS : ROWS - SLOTS, :] = about.astype(BF16)
    copies = []
    for i in range(4):
        count = lax.dot_general(
            onehot(128, slot, i * 128), picks, NT, preferred_element_type=F32
        )
        low, high = split_count(count)
        sums = dot(low.astype(BF16), feats) + dot((high * 256.0).astype(BF16), feats)
        sums = sums.astype(BF16)
        for t in range(4):
            for k in range(4):
                mid_ref[i * 4 + t, 32 * k : 32 * k + 32, :] = sums[
                    t * 32 : (t + 1) * 32, k * 128 : (k + 1) * 128
                ]
        copies.append(
            pltpu.make_async_copy(
                mid_ref.at[pl.ds(4 * i, 4)],
                mid_hbm.at[pl.ds(4 * i, 4), pl.ds(SLOTS, ROWS - SLOTS)],
                out_sems.at[i],
            )
        )
        copies[-1].start()
    for copy in copies:
        copy.wait()


def fill_body(rows_0, rows_1, mid_in, mid_ref, wide, block, sem):
    del mid_in
    for k, rows in enumerate((rows_0, rows_1)):
        wide[4 * k : 4 * k + 4, :] = rows[...].astype(F32)
    for k in range(4):
        part = wide[:, 128 * k : 128 * k + 128].astype(BF16)
        for t in range(16):
            block[t, 8 * k : 8 * k + 8, :] = part
    copy = pltpu.make_async_copy(block, mid_ref.at[:, pl.ds(GATHERED, 32)], sem)
    copy.start()
    copy.wait()


def reduce_body(mid_ref, out_hbm, table_ref, out_ref, sem):
    lane = lax.broadcasted_iota(I32, (8, 128), 1)
    blocks = []
    for k in range(4):
        block = jnp.zeros((8, 128), F32)
        for i in range(4):
            block = jnp.where(lane >> 5 == i, mid_ref[4 * k + i, ABOUT:ROWS, :].astype(F32), block)
        blocks.append(block)
    about = jnp.concatenate(blocks, axis=1)
    count = about[0:1] + 256.0 * about[1:2]
    lane = lax.broadcasted_iota(I32, (1, 512), 1)
    target = ((lane & 31) >> 1) * 4 + about[2:3].astype(I32)
    picks = onehot(64, target)
    slots = [mid_ref[:, block_of(SLOTS, k), :].reshape(512, 128) for k in range(4)]
    sums = dot(picks, jnp.concatenate(slots, axis=1))
    degree = jnp.sum(picks.astype(F32) * count, axis=1, keepdims=True)
    low, high = split_count(degree)
    extra_lane = lax.broadcasted_iota(I32, (64, 128), 1)
    extra = jnp.where(extra_lane == 0, low, jnp.where(extra_lane == 1, high, 0.0))
    for g in range(16):
        out_ref[g, :, 0:512] = sums[4 * g : 4 * g + 4].astype(BF16)
        out_ref[g, :, 512:640] = extra[4 * g : 4 * g + 4].astype(BF16)
    copy = pltpu.make_async_copy(out_ref, out_hbm, sem)
    copy.start()
    for k in range(4):
        table_ref[:, 128 * k : 128 * k + 128] = mid_ref[:, block_of(GATHERED, k), :].reshape(128, 128)
    copy.wait()


def counts_body(
    where_ref, src_ref, dst_ref, feats_ref, hub_ref, weight_ref,
    low_ref, high_ref, degree_ref, hub_linear_ref, partial_ref,
):
    core = where_ref[0]
    side = where_ref[1]
    near = where_ref[2]
    far = where_ref[3]
    src = src_ref[...]
    targets = onehot(128, dst_ref[...])
    hub = src - 160
    table = (((hub >> 2) & 1) ^ core) * 4 + (((hub >> 5) & 1) ^ far) * 2
    table = table + (((hub >> 3) & 1) ^ side)
    column = table * 128 + (hub >> 6) * 8 + (((hub >> 4) & 1) ^ near) * 4 + (hub & 3)
    column = jnp.where(hub < 0, -1, column)
    degree_ref[...] = jnp.broadcast_to(
        jnp.sum(targets.astype(F32), axis=1, keepdims=True), degree_ref.shape
    )

    def counted(index, first):
        count = lax.dot_general(
            targets, onehot(256, index, first), NT, preferred_element_type=F32
        )
        low, high = split_count(count)
        return low.astype(BF16), (high * 256.0).astype(BF16)

    def chunk(i, carry):
        low, high = counted(column, i * 256)
        place = pl.ds(pl.multiple_of(i * 256, 256), 256)
        low_ref[:, place] = low
        high_ref[:, place] = high
        return carry

    lax.fori_loop(0, 4, chunk, 0)
    total = jnp.zeros((128, 512), F32)
    for part, ref in zip(counted(src, 0), (low_ref, high_ref)):
        total = total + dot(part[:, 0:128], feats_ref[...])
        ref[:, 1024:1152] = part[:, 128:256]
    partial_ref[...] = total
    hub_linear_ref[...] = dot(hub_ref[...], weight_ref[0:512])


def nodes_body(
    low_ref, high_ref, partial_ref, feats_ref, before_ref, after_ref,
    table_0, table_1, table_2, table_3, weight_ref,
    total_ref, linear_ref,
):
    linear_ref[...] = dot(feats_ref[...], weight_ref[0:512])
    total = partial_ref[...]
    tables = jnp.concatenate([t[...] for t in (table_0, table_1, table_2, table_3)], axis=0)
    for ref in (low_ref, high_ref):
        total = total + dot(ref[:, 1024:1040], before_ref[...])
        total = total + dot(ref[:, 1040:1056], after_ref[...])
        total = total + dot(ref[:, 0:512], tables)
    total_ref[...] = total


def finish_body(
    low_ref, high_ref, degree_ref, total_ref, linear_ref,
    table_4, table_5, table_6, table_7, weight_ref, out_ref,
):
    total = total_ref[...]
    tables = jnp.concatenate([t[...] for t in (table_4, table_5, table_6, table_7)], axis=0)
    for ref in (low_ref, high_ref):
        total = total + dot(ref[:, 512:1024], tables)
    mean = (total / degree_ref[:, 0:1]).astype(BF16)
    out_ref[...] = normalized(linear_ref[...] + dot(mean, weight_ref[512:1024]))


def hubs_body(parts_ref, linear_ref, weight_ref, out_ref):
    total = jnp.zeros((4, 640), F32)
    for g in range(16):
        total = total + parts_ref[g].astype(F32)
    degree = total[:, 512:513] + 256.0 * total[:, 513:514]
    mean = (total[:, 0:512] / degree).astype(BF16)
    out_ref[...] = normalized(linear_ref[...] + dot(mean, weight_ref[512:1024]))


VMEM = pl.BlockSpec(memory_space=pltpu.VMEM)
SMEM = pl.BlockSpec(memory_space=pltpu.SMEM)
ANY = pl.BlockSpec(memory_space=pl.ANY)
HBM = pl.BlockSpec(memory_space=pltpu.HBM)


def call(body, out, specs, flops, nbytes, limit=16, **more):
    out_specs = more.pop("out_specs", jax.tree.map(lambda _: VMEM, out))
    return pl.pallas_call(
        body,
        out_shape=out,
        in_specs=specs,
        out_specs=out_specs,
        compiler_params=pltpu.CompilerParams(vmem_limit_bytes=limit * MIB),
        cost_estimate=pl.CostEstimate(flops=flops, bytes_accessed=nbytes, transcendentals=0),
        **more,
    )


def shape(*dims, dtype=BF16):
    return jax.ShapeDtypeStruct(dims, dtype)


def in_hbm(*arrays):
    return [pltpu.with_memory_space_constraint(a, pltpu.HBM) for a in arrays]


def on_device(
    node_feats, hub_feats, weight, edge_src, edge_dst, bound_rows,
    hub_edge_src, hub_edge_slot, slot_hub,
):
    axes = ("core", "side", "near", "far")
    where = jnp.stack([lax.axis_index(axis) for axis in axes]).astype(I32)
    swap = [(0, 1), (1, 0)]
    gathered = lax.ppermute(hub_feats, "near", swap)
    mid = call(
        slots_body, pltpu.HBM((16, ROWS, 128), BF16), [HBM] * 4, 1 << 30, 2 << 20,
        out_specs=HBM,
        scratch_shapes=[
            pltpu.VMEM((1, 1024), I32),
            pltpu.VMEM((1, 1024), I32),
            pltpu.VMEM((1, 512), I32),
            pltpu.VMEM((128, 512), BF16),
            pltpu.SemaphoreType.DMA((4,)),
            pltpu.VMEM((16, ROWS - SLOTS, 128), BF16),
            pltpu.SemaphoreType.DMA((4,)),
        ],
    )(*in_hbm(hub_edge_src, hub_edge_slot, slot_hub, node_feats))
    mid = call(
        fill_body, pltpu.HBM((16, ROWS, 128), BF16), [VMEM] * 2 + [HBM], 0, 1 << 20,
        out_specs=HBM,
        input_output_aliases={2: 0},
        scratch_shapes=[
            pltpu.VMEM((8, 512), F32),
            pltpu.VMEM((16, 32, 128), BF16),
            pltpu.SemaphoreType.DMA,
        ],
    )(hub_feats, gathered, mid)
    mid = lax.all_to_all(mid, OUTER, 0, 0, tiled=True)
    exports = call(export_body, shape(16, 512), [VMEM] * 2, 2 << 20, 150000)(bound_rows, node_feats)
    count = lax.axis_size(DOM)
    forward = [(i, (i + 1) % count) for i in range(count)]
    backward = [(target, source) for source, target in forward]
    before = lax.ppermute(exports, DOM, forward)
    after = lax.ppermute(exports, DOM, backward)
    low, high, degree, hub_linear, partial = call(
        counts_body,
        (
            shape(128, 1152), shape(128, 1152), shape(128, 128, dtype=F32),
            shape(4, 512, dtype=F32), shape(128, 512, dtype=F32),
        ),
        [SMEM] + [VMEM] * 5, 1 << 30, 2 << 20,
    )(where, edge_src, edge_dst, node_feats, hub_feats, weight)
    parts, table_0 = call(
        reduce_body, (pltpu.HBM((16, 4, 640), BF16), shape(128, 512)), [VMEM],
        1 << 26, 2 << 20,
        out_specs=(HBM, VMEM),
        scratch_shapes=[pltpu.VMEM((16, 4, 640), BF16), pltpu.SemaphoreType.DMA],
    )(mid)
    table_1 = lax.ppermute(table_0, "side", swap)
    table_2 = lax.ppermute(table_0, "far", swap)
    table_3 = lax.ppermute(table_0, ("far", "side"), [(i, i ^ 3) for i in range(4)])
    parts = lax.all_to_all(parts, INNER, 0, 0, tiled=True)
    tables = [table_0, table_1, table_2, table_3]
    others = []
    for table in tables:
        others.append(lax.ppermute(table, "core", swap))
    wide = shape(128, 512, dtype=F32)
    total, linear = call(nodes_body, (wide, wide), [VMEM] * 11, 1 << 28, 1 << 20)(
        low, high, partial, node_feats, before, after, *tables, weight
    )
    node_out = call(finish_body, shape(128, 512), [VMEM] * 10, 1 << 28, 1 << 20)(
        low, high, degree, total, linear, *others, weight
    )
    hub_out = call(hubs_body, shape(4, 512), [VMEM] * 3, 1 << 22, 1 << 19)(
        parts, hub_linear, weight
    )
    return (node_out, hub_out)


def solution(mesh):
    finer = Mesh(mesh.devices.reshape(4, 4, 2, 2, 2, 2), ROLE_DOM)
    rows = P(ROLE_DOM, None)
    in_specs = (rows, rows, P(), rows, rows, rows, rows, rows, rows)
    return jax.shard_map(
        on_device, mesh=finer, in_specs=in_specs, out_specs=(rows, rows), check_vma=False
    )
```

```python
import jax
import jax.numpy as jnp
from jax import lax
from jax.experimental import pallas as pl
from jax.experimental.pallas import tpu as pltpu
from jax.sharding import Mesh
from jax.sharding import PartitionSpec as P


Z = ("far", "near", "side")
INNER = ("far", "near", "side", "core")
OUTER = ("role", "x")
DOM = ("x", "far", "near", "side", "core")
ROLE_DOM = ("role", "x", "far", "near", "side", "core")

epsilon = 1e-06
F32 = jnp.float32
BF16 = jnp.bfloat16
I32 = jnp.int32
NT = (((1,), (1,)), ((), ()))
TN = (((0,), (0,)), ((), ()))
MIB = 1 << 20


def dot(a, b):
    return jnp.dot(a, b, preferred_element_type=F32)


def onehot(rows, index, first=0):
    shape = (rows, index.shape[1])
    row = lax.broadcasted_iota(jnp.int16, shape, 0)
    place = jnp.broadcast_to(index - first, shape).astype(jnp.int16)
    return jnp.where(row == place, jnp.ones(shape, BF16), jnp.zeros(shape, BF16))


def split_count(count):
    high = jnp.floor(count * (1.0 / 256.0))
    return count - high * 256.0, high


def normalized(linear):
    rectified = jnp.maximum(linear, 0.0)
    mean = jnp.mean(rectified * rectified, axis=1, keepdims=True)
    return (rectified * lax.rsqrt(mean + epsilon)).astype(BF16)


def export_body(bound_ref, feats_ref, out_ref):
    picks = onehot(feats_ref.shape[0], bound_ref[...])
    out_ref[...] = lax.dot_general(picks, feats_ref[...], TN, preferred_element_type=F32).astype(BF16)


def repeated(index):
    shape = (128, index.shape[1])
    row = lax.broadcasted_iota(I32, shape, 0) & 31
    return jnp.where(row == index, 1.0, 0.0).astype(BF16)


GATHERED, SLOTS, ABOUT, ROWS = 0, 32, 160, 168


def block_of(first, k):
    size = (SLOTS if first == GATHERED else ABOUT - SLOTS) // 4
    return pl.ds(first + size * k, size)


def slots_body(
    src_hbm, slot_hbm, hub_hbm, feats_hbm, mid_hbm,
    src_ref, slot_ref, hub_ref, feats_ref, sems, mid_ref, out_sems,
):
    copies = [
        pltpu.make_async_copy(source, target, sems.at[k])
        for k, (source, target) in enumerate(
            ((src_hbm, src_ref), (slot_hbm, slot_ref), (hub_hbm, hub_ref), (feats_hbm, feats_ref))
        )
    ]
    for copy in copies:
        copy.start()
    for copy in copies:
        copy.wait()
    feats = feats_ref[...]
    slot = slot_ref[...]
    picks = onehot(128, src_ref[...])
    count = lax.dot_general(
        onehot(16, slot >> 5), repeated(slot & 31), NT, preferred_element_type=F32
    )
    low, high = split_count(count)
    lane = lax.broadcasted_iota(I32, (1, 512), 1)
    hubs = hub_ref[...].astype(F32)
    which = (onehot(16, lane >> 5).astype(F32) * hubs).astype(BF16)
    hub = lax.dot_general(which, repeated(lane & 31), NT, preferred_element_type=F32)
    row = lax.broadcasted_iota(I32, (8, 128), 0)
    for t in range(16):
        about = jnp.where(row == 0, low[t : t + 1], 0.0)
        about = jnp.where(row == 1, high[t : t + 1], about)
        about = jnp.where(row == 2, hub[t : t + 1], about)
        mid_ref[t, ABOUT - SLOTS : ROWS - SLOTS, :] = about.astype(BF16)
    copies = []
    for i in range(4):
        count = lax.dot_general(
            onehot(128, slot, i * 128), picks, NT, preferred_element_type=F32
        )
        low, high = split_count(count)
        sums = dot(low.astype(BF16), feats) + dot((high * 256.0).astype(BF16), feats)
        sums = sums.astype(BF16)
        for t in range(4):
            for k in range(4):
                mid_ref[i * 4 + t, 32 * k : 32 * k + 32, :] = sums[
                    t * 32 : (t + 1) * 32, k * 128 : (k + 1) * 128
                ]
        copies.append(
            pltpu.make_async_copy(
                mid_ref.at[pl.ds(4 * i, 4)],
                mid_hbm.at[pl.ds(4 * i, 4), pl.ds(SLOTS, ROWS - SLOTS)],
                out_sems.at[i],
            )
        )
        copies[-1].start()
    for copy in copies:
        copy.wait()


def fill_body(rows_0, rows_1, mid_in, mid_ref, wide, block, sem):
    del mid_in
    for k, rows in enumerate((rows_0, rows_1)):
        wide[4 * k : 4 * k + 4, :] = rows[...].astype(F32)
    for k in range(4):
        part = wide[:, 128 * k : 128 * k + 128].astype(BF16)
        for t in range(16):
            block[t, 8 * k : 8 * k + 8, :] = part
    copy = pltpu.make_async_copy(block, mid_ref.at[:, pl.ds(GATHERED, 32)], sem)
    copy.start()
    copy.wait()


def reduce_body(mid_ref, out_hbm, table_ref, out_ref, sem):
    lane = lax.broadcasted_iota(I32, (8, 128), 1)
    blocks = []
    for k in range(4):
        block = jnp.zeros((8, 128), F32)
        for i in range(4):
            block = jnp.where(lane >> 5 == i, mid_ref[4 * k + i, ABOUT:ROWS, :].astype(F32), block)
        blocks.append(block)
    about = jnp.concatenate(blocks, axis=1)
    count = about[0:1] + 256.0 * about[1:2]
    lane = lax.broadcasted_iota(I32, (1, 512), 1)
    target = ((lane & 31) >> 1) * 4 + about[2:3].astype(I32)
    picks = onehot(64, target)
    slots = [mid_ref[:, block_of(SLOTS, k), :].reshape(512, 128) for k in range(4)]
    sums = dot(picks, jnp.concatenate(slots, axis=1))
    degree = jnp.sum(picks.astype(F32) * count, axis=1, keepdims=True)
    low, high = split_count(degree)
    extra_lane = lax.broadcasted_iota(I32, (64, 128), 1)
    extra = jnp.where(extra_lane == 0, low, jnp.where(extra_lane == 1, high, 0.0))
    for g in range(16):
        out_ref[g, :, 0:512] = sums[4 * g : 4 * g + 4].astype(BF16)
        out_ref[g, :, 512:640] = extra[4 * g : 4 * g + 4].astype(BF16)
    copy = pltpu.make_async_copy(out_ref, out_hbm, sem)
    copy.start()
    for k in range(4):
        table_ref[:, 128 * k : 128 * k + 128] = mid_ref[:, block_of(GATHERED, k), :].reshape(128, 128)
    copy.wait()


def counts_body(
    where_ref, src_ref, dst_ref, feats_ref, hub_ref, weight_ref,
    low_ref, high_ref, degree_ref, hub_linear_ref, partial_ref,
):
    core = where_ref[0]
    z = where_ref[1]
    src = src_ref[...]
    targets = onehot(128, dst_ref[...])
    hub = src - 160
    ahead = ((hub >> 3) - z) & 7
    turn = ahead >> 1
    table = jnp.where(turn > 1, 5 - turn, turn)
    part = ahead & 1
    table = table + (((hub >> 2) & 1) ^ core) * 4
    column = table * 128 + (hub >> 6) * 8 + part * 4 + (hub & 3)
    column = jnp.where(hub < 0, -1, column)
    degree_ref[...] = jnp.broadcast_to(
        jnp.sum(targets.astype(F32), axis=1, keepdims=True), degree_ref.shape
    )

    def counted(index, first):
        count = lax.dot_general(
            targets, onehot(256, index, first), NT, preferred_element_type=F32
        )
        low, high = split_count(count)
        return low.astype(BF16), (high * 256.0).astype(BF16)

    def chunk(i, carry):
        low, high = counted(column, i * 256)
        place = pl.ds(pl.multiple_of(i * 256, 256), 256)
        low_ref[:, place] = low
        high_ref[:, place] = high
        return carry

    lax.fori_loop(0, 4, chunk, 0)
    total = jnp.zeros((128, 512), F32)
    for part, ref in zip(counted(src, 0), (low_ref, high_ref)):
        total = total + dot(part[:, 0:128], feats_ref[...])
        ref[:, 1024:1152] = part[:, 128:256]
    partial_ref[...] = total
    hub_linear_ref[...] = dot(hub_ref[...], weight_ref[0:512])


def nodes_body(
    low_ref, high_ref, partial_ref, feats_ref, before_ref, after_ref,
    table_0, table_1, table_2, table_3, weight_ref,
    total_ref, linear_ref,
):
    linear_ref[...] = dot(feats_ref[...], weight_ref[0:512])
    total = partial_ref[...]
    tables = jnp.concatenate([t[...] for t in (table_0, table_1, table_2, table_3)], axis=0)
    for ref in (low_ref, high_ref):
        total = total + dot(ref[:, 1024:1040], before_ref[...])
        total = total + dot(ref[:, 1040:1056], after_ref[...])
        total = total + dot(ref[:, 0:512], tables)
    total_ref[...] = total


def finish_body(
    low_ref, high_ref, degree_ref, total_ref, linear_ref,
    table_4, table_5, table_6, table_7, weight_ref, out_ref,
):
    total = total_ref[...]
    tables = jnp.concatenate([t[...] for t in (table_4, table_5, table_6, table_7)], axis=0)
    for ref in (low_ref, high_ref):
        total = total + dot(ref[:, 512:1024], tables)
    mean = (total / degree_ref[:, 0:1]).astype(BF16)
    out_ref[...] = normalized(linear_ref[...] + dot(mean, weight_ref[512:1024]))


def hubs_body(parts_ref, linear_ref, weight_ref, out_ref):
    total = jnp.zeros((4, 640), F32)
    for g in range(16):
        total = total + parts_ref[g].astype(F32)
    degree = total[:, 512:513] + 256.0 * total[:, 513:514]
    mean = (total[:, 0:512] / degree).astype(BF16)
    out_ref[...] = normalized(linear_ref[...] + dot(mean, weight_ref[512:1024]))


VMEM = pl.BlockSpec(memory_space=pltpu.VMEM)
SMEM = pl.BlockSpec(memory_space=pltpu.SMEM)
ANY = pl.BlockSpec(memory_space=pl.ANY)
HBM = pl.BlockSpec(memory_space=pltpu.HBM)


def call(body, out, specs, flops, nbytes, limit=16, **more):
    out_specs = more.pop("out_specs", jax.tree.map(lambda _: VMEM, out))
    return pl.pallas_call(
        body,
        out_shape=out,
        in_specs=specs,
        out_specs=out_specs,
        compiler_params=pltpu.CompilerParams(vmem_limit_bytes=limit * MIB),
        cost_estimate=pl.CostEstimate(flops=flops, bytes_accessed=nbytes, transcendentals=0),
        **more,
    )


def shape(*dims, dtype=BF16):
    return jax.ShapeDtypeStruct(dims, dtype)


def in_hbm(*arrays):
    return [pltpu.with_memory_space_constraint(a, pltpu.HBM) for a in arrays]


def on_device(
    node_feats, hub_feats, weight, edge_src, edge_dst, bound_rows,
    hub_edge_src, hub_edge_slot, slot_hub,
):
    where = jnp.stack([lax.axis_index("core"), lax.axis_index(Z)]).astype(I32)
    swap = [(0, 1), (1, 0)]
    planes = lax.axis_size(Z)

    def from_plane(value, step):
        return lax.ppermute(value, Z, [(i, (i - step) % planes) for i in range(planes)])

    gathered = from_plane(hub_feats, 1)
    mid = call(
        slots_body, pltpu.HBM((16, ROWS, 128), BF16), [HBM] * 4, 1 << 30, 2 << 20,
        out_specs=HBM,
        scratch_shapes=[
            pltpu.VMEM((1, 1024), I32),
            pltpu.VMEM((1, 1024), I32),
            pltpu.VMEM((1, 512), I32),
            pltpu.VMEM((128, 512), BF16),
            pltpu.SemaphoreType.DMA((4,)),
            pltpu.VMEM((16, ROWS - SLOTS, 128), BF16),
            pltpu.SemaphoreType.DMA((4,)),
        ],
    )(*in_hbm(hub_edge_src, hub_edge_slot, slot_hub, node_feats))
    mid = call(
        fill_body, pltpu.HBM((16, ROWS, 128), BF16), [VMEM] * 2 + [HBM], 0, 1 << 20,
        out_specs=HBM,
        input_output_aliases={2: 0},
        scratch_shapes=[
            pltpu.VMEM((8, 512), F32),
            pltpu.VMEM((16, 32, 128), BF16),
            pltpu.SemaphoreType.DMA,
        ],
    )(hub_feats, gathered, mid)
    mid = lax.all_to_all(mid, OUTER, 0, 0, tiled=True)
    exports = call(export_body, shape(16, 512), [VMEM] * 2, 2 << 20, 150000)(bound_rows, node_feats)
    count = lax.axis_size(DOM)
    forward = [(i, (i + 1) % count) for i in range(count)]
    backward = [(target, source) for source, target in forward]
    before = lax.ppermute(exports, DOM, forward)
    after = lax.ppermute(exports, DOM, backward)
    low, high, degree, hub_linear, partial = call(
        counts_body,
        (
            shape(128, 1152), shape(128, 1152), shape(128, 128, dtype=F32),
            shape(4, 512, dtype=F32), shape(128, 512, dtype=F32),
        ),
        [SMEM] + [VMEM] * 5, 1 << 30, 2 << 20,
    )(where, edge_src, edge_dst, node_feats, hub_feats, weight)
    parts, table_0 = call(
        reduce_body, (pltpu.HBM((16, 4, 640), BF16), shape(128, 512)), [VMEM],
        1 << 26, 2 << 20,
        out_specs=(HBM, VMEM),
        scratch_shapes=[pltpu.VMEM((16, 4, 640), BF16), pltpu.SemaphoreType.DMA],
    )(mid)
    table_1 = from_plane(table_0, 2)
    table_2 = from_plane(table_0, -2)
    table_3 = from_plane(table_0, 4)
    parts = lax.all_to_all(parts, INNER, 0, 0, tiled=True)
    tables = [table_0, table_1, table_2, table_3]
    others = []
    for table in tables:
        others.append(lax.ppermute(table, "core", swap))
    wide = shape(128, 512, dtype=F32)
    total, linear = call(nodes_body, (wide, wide), [VMEM] * 11, 1 << 28, 1 << 20)(
        low, high, partial, node_feats, before, after, *tables, weight
    )
    node_out = call(finish_body, shape(128, 512), [VMEM] * 10, 1 << 28, 1 << 20)(
        low, high, degree, total, linear, *others, weight
    )
    hub_out = call(hubs_body, shape(4, 512), [VMEM] * 3, 1 << 22, 1 << 19)(
        parts, hub_linear, weight
    )
    return (node_out, hub_out)


def solution(mesh):
    finer = Mesh(mesh.devices.reshape(4, 4, 2, 2, 2, 2), ROLE_DOM)
    rows = P(ROLE_DOM, None)
    in_specs = (rows, rows, P(), rows, rows, rows, rows, rows, rows)
    return jax.shard_map(
        on_device, mesh=finer, in_specs=in_specs, out_specs=(rows, rows), check_vma=False
    )
```
